512 devices in a mesh: head: 8 (over x, core), ctx: 64 (over z, y).
Axes of the slice: x: 4, y: 8, z: 8, core: 2. Of those that a mesh axis runs over, the one named last changes fastest.
Arguments:
- queries: bfloat16 [8192, 6144], P('ctx', 'head'), may hold values from -6 to 6
- key_rows: bfloat16 [8192, 1024], P('ctx', 'head'), may hold values from -6 to 6
- value_rows: bfloat16 [8192, 1024], P('ctx', 'head'), may hold values from -6 to 6
- out_grad: bfloat16 [8192, 6144], P('ctx', 'head'), may hold values from -24 to 24
- gate_logit: float32 [8192], P('ctx'), may hold values from -6 to 6
- tile_plan: int32 [64, 4, 64], replicated, may hold values from -1 to 15, as said below
- mask_kind: int32 [64, 4, 64], P('ctx'), may hold values from 0 to 1
Outputs:
- query_grad: bfloat16 [8192, 6144], P('ctx', 'head')
- key_grad: bfloat16 [8192, 1024], P('ctx', 'head')
- value_grad: bfloat16 [8192, 1024], P('ctx', 'head')
- gate_grad: float32 [8192], P('ctx')
The draws below stay inside these ranges and needn't reach their ends.
Inputs may be any that keep to these rules, and one draw needn't show every extreme that they name: tile_plan[b, s, p] is a key tile of block p (of 8 rows) that block b reads in section s, or -1; it is -1 when p == b; the tiles that b reads from one p differ from section to section; in every section each block reads from between 16 and 32 blocks, and some block reads from exactly 32.
All inputs are finite; a program needn't handle non-finite values.
Results may differ from the reference program's by a relative error of at most 0.033.
Values may be sent and summed in bfloat16 or wider, within the bound.
No kernel may reach another device: no remote copies, remote signals or barrier semaphores. Data moves between devices by JAX's collectives and lax.ppermute only.
A program may use at most 64 MiB of HBM per device.

```python
import math
import jax
import jax.numpy as jnp
from jax import lax

QH = 48
KVH = 8
HD = 128
ROWS = 128
TILE = 8
SECTIONS = 4
SEQ = 8192
PICKS = 32
N_CTX = 64


def draw_queries(key, part):
    blocks = SEQ // ROWS
    base_key = jax.random.fold_in(key, 11)
    field = jnp.clip(jax.random.normal(base_key, (SEQ, QH * HD), jnp.float32), -6.0, 6.0)
    field = field.reshape(blocks, ROWS, QH * HD)
    return field.reshape(SEQ, QH * HD).astype(jnp.bfloat16)


def draw_key_rows(key, part):
    blocks = SEQ // ROWS
    base_key = jax.random.fold_in(key, 12)
    field = jnp.clip(jax.random.normal(base_key, (SEQ, KVH * HD), jnp.float32), -6.0, 6.0)
    field = field.reshape(blocks, ROWS, KVH * HD)
    return field.reshape(SEQ, KVH * HD).astype(jnp.bfloat16)


def draw_out_grad(key, part):
    columns = QH * HD
    base_key = jax.random.fold_in(key, 13)
    field = jnp.clip(jax.random.normal(base_key, (SEQ, columns), jnp.float32), -4.0, 4.0)
    ratio = 3.0
    rough = jnp.exp(jax.random.uniform(jax.random.fold_in(key, 15), (columns,), jnp.float32, -0.35, 0.35))
    rising = ratio ** (jnp.arange(columns).astype(jnp.float32) / (columns - 1))
    return (field * rising[None, :] * rough[None, :]).astype(jnp.bfloat16)


def draw_tile_plan(key, part):
    blocks = SEQ // ROWS
    tile_count = ROWS // TILE
    first, second, third, fourth = jax.random.split(jax.random.fold_in(key, 14), 4)
    block_index = jnp.arange(blocks, dtype=jnp.int32)
    scores = jax.random.randint(first, (blocks, SECTIONS, blocks), 0, 1 << 20) * blocks + block_index[None, None, :]
    itself = block_index[:, None, None] == block_index[None, None, :]
    scores = jnp.where(itself, (1 << 20) * blocks + blocks, scores)
    ranking = jnp.argsort(jnp.argsort(scores, axis=-1), axis=-1)
    counts = jax.random.randint(second, (blocks, SECTIONS), blocks // 4, blocks // 2 + 1)
    filled = jax.random.randint(third, (SECTIONS,), 0, blocks)
    counts = jnp.where(block_index[:, None] == filled[None, :], blocks // 2, counts)
    chosen = ranking < counts[:, :, None]
    tile_scores = jax.random.randint(fourth, (blocks, blocks, tile_count), 0, 1 << 20) * tile_count + jnp.arange(tile_count)[None, None, :]
    tile_order = jnp.argsort(tile_scores, axis=-1)[:, :, :SECTIONS]
    tile_pick = jnp.transpose(tile_order, (0, 2, 1))
    return jnp.where(chosen, tile_pick, -1).astype(jnp.int32)


def place_ends(values, stream_key, low, largest):
    longest = values.shape.index(max(values.shape))
    spots = []
    for shift in (0, 1):
        where = [jax.random.randint(jax.random.fold_in(stream_key, axis), (), 0, length) for axis, length in enumerate(values.shape)]
        where[longest] = (where[longest] + shift) % values.shape[longest]
        spots.append(tuple(where))
    return values.at[spots[0]].set(low).at[spots[1]].set(largest)


def block_levels(own_key, extent, cuts, low, top_value):
    def one(axis_at, parts):
        heights = jax.random.uniform(jax.random.fold_in(jax.random.fold_in(own_key, 6), axis_at), (parts,), jnp.float32, low / len(cuts), top_value / len(cuts))
        return jnp.repeat(jnp.exp(heights), extent[axis_at] // parts).reshape((-1,) + (1,) * (len(extent) - axis_at - 1))

    gain = one(*cuts[0])
    for cut in cuts[1:]:
        gain = gain * one(*cut)
    return gain


def centred(rng, shape, scale, limit, pieces=(), kind=jnp.bfloat16):
    result = jax.random.normal(rng, shape, jnp.float32) * scale
    if len(pieces) > 0:
        result = block_levels(rng, shape, pieces, -0.22, 0.18) * result
    return jnp.clip(result, min=-limit, max=limit).astype(kind)


def setup_inputs(seed: int = 0) -> dict:
    key_list = jax.random.split(jax.random.key(seed), 8)
    return {
        "queries": draw_queries(jax.random.fold_in(key_list[7], 71), 0),
        "key_rows": draw_key_rows(jax.random.fold_in(key_list[7], 71), 0),
        "value_rows": centred(key_list[2], (SEQ, KVH * HD), 1.0, 6.0, ((0, 64), (1, 8))),
        "out_grad": draw_out_grad(jax.random.fold_in(key_list[7], 71), 0),
        "gate_logit": centred(key_list[4], (SEQ,), 1.5, 6.0, ((0, 64),), jnp.float32),
        "tile_plan": draw_tile_plan(jax.random.fold_in(key_list[7], 71), 0),
        "mask_kind": place_ends(jax.random.randint(key_list[6], (N_CTX, SECTIONS, N_CTX), 0, 2), jax.random.fold_in(key_list[6], 1), 0, 1).astype(jnp.int32),
    }


big_negative = -1e+30

def rounded(values):
    return lax.optimization_barrier(values.astype(jnp.bfloat16)).astype(jnp.float32)

def reference(queries, key_rows, value_rows, out_grad, gate_logit, tile_plan, mask_kind):
    blocks = SEQ // ROWS
    group_size = QH // KVH
    factor = 1.0 / math.sqrt(HD)
    gate = jax.nn.sigmoid(gate_logit.astype(jnp.float32))
    row_index = jnp.arange(ROWS, dtype=jnp.int32)
    tile_rows = jnp.arange(TILE, dtype=jnp.int32)
    late_rows = row_index >= ROWS // 2
    causal = row_index[:, None] >= row_index[None, :]
    key_float = key_rows.astype(jnp.float32).reshape(SEQ, KVH, HD)
    value_float = value_rows.astype(jnp.float32).reshape(SEQ, KVH, HD)

    def per_block(carry, index):
        key_total, value_total = carry
        start = (index * ROWS).astype(jnp.int32)
        query_block = lax.dynamic_slice_in_dim(queries, start, ROWS, 0).astype(jnp.float32).reshape(ROWS, KVH, group_size, HD)
        grad_block = lax.dynamic_slice_in_dim(out_grad, start, ROWS, 0).astype(jnp.float32).reshape(ROWS, KVH, group_size, HD)
        gate_block = lax.dynamic_slice_in_dim(gate, start, ROWS, 0)
        plan_row = tile_plan[index]
        kind_row = mask_kind[index]
        slot_order = jnp.argsort((plan_row < 0).astype(jnp.int32), axis=1, stable=True)[:, :PICKS].astype(jnp.int32)
        slot_tiles = jnp.take_along_axis(plan_row, slot_order, axis=1)
        slot_kinds = jnp.take_along_axis(kind_row, slot_order, axis=1)
        remote_rows = (slot_order * ROWS + jnp.maximum(slot_tiles, 0) * TILE)[:, :, None] + tile_rows
        all_rows = jnp.concatenate([start + row_index, remote_rows.reshape(-1).astype(jnp.int32)]).astype(jnp.int32)
        key_block = key_float[all_rows]
        value_block = value_float[all_rows]
        seen_tile = (slot_tiles >= 0)[None] & ((slot_kinds == 0)[None] | late_rows[:, None, None])
        seen_remote = jnp.broadcast_to(seen_tile[..., None], (ROWS, SECTIONS, PICKS, TILE)).reshape(ROWS, -1)
        visible = jnp.concatenate([causal, seen_remote], axis=1)
        scores = jnp.einsum('rcgd,kcd->cgrk', query_block, key_block) * factor
        masked = jnp.where(visible[None, None], scores, big_negative)
        highest = lax.optimization_barrier(jnp.max(masked, axis=-1, keepdims=True))
        log_total = highest + jnp.log(lax.optimization_barrier(jnp.sum(jnp.exp(masked - highest), axis=-1, keepdims=True)))
        probs = jnp.exp(masked - log_total)
        probs_low = rounded(probs)
        attended = rounded(jnp.einsum('cgrk,kcd->rcgd', probs_low, value_block))
        gate_sum = lax.optimization_barrier(jnp.sum(grad_block * attended, axis=(1, 2, 3)))
        gate_part = gate_block * (1.0 - gate_block) * gate_sum
        d_attended = rounded(gate_block[:, None, None, None] * grad_block)
        delta = jnp.transpose(lax.optimization_barrier(jnp.sum(d_attended * attended, axis=-1)), (1, 2, 0))
        d_probs = jnp.einsum('rcgd,kcd->cgrk', d_attended, value_block)
        d_scores = rounded(probs * (d_probs - delta[..., None]))
        query_part = jnp.einsum('cgrk,kcd->rcgd', d_scores, key_block) * factor
        key_part = jnp.einsum('cgrk,rcgd->kcd', d_scores, query_block) * factor
        value_part = jnp.einsum('cgrk,rcgd->kcd', probs_low, d_attended)
        key_total = key_total.at[all_rows].add(key_part.reshape(-1, KVH * HD))
        value_total = value_total.at[all_rows].add(value_part.reshape(-1, KVH * HD))
        query_out = query_part.reshape(ROWS, QH * HD).astype(jnp.bfloat16)
        return ((key_total, value_total), (query_out, gate_part))
    zeros_total = jnp.zeros((SEQ, KVH * HD), jnp.float32)
    totals, outputs = lax.scan(per_block, (zeros_total, zeros_total), jnp.arange(blocks, dtype=jnp.int32))
    query_grad = outputs[0].reshape(SEQ, QH * HD)
    gate_grad = outputs[1].reshape(SEQ)
    return (query_grad, totals[0].astype(jnp.bfloat16), totals[1].astype(jnp.bfloat16), gate_grad)
```

```python
import math

import jax
import jax.numpy as jnp
from jax import lax
from jax.experimental import pallas as pl
from jax.experimental.pallas import tpu as pltpu
from jax.sharding import PartitionSpec as P

HD = 128
TILE = 8
SECTIONS = 4
ROWS = 128
PEERS = 64
GROUP = 6
SLOTS = PEERS * SECTIONS
KEYS = SLOTS * TILE
WIDE = GROUP * ROWS
CHUNK = 256
N_CHUNK = KEYS // CHUNK
FACTOR = 1.0 / math.sqrt(HD)
SCALE = FACTOR * math.log2(math.e)
HIDDEN = -1e30
INTERPRET = False
VMEM_LIMIT = 40 * 1024 * 1024

f32 = jnp.float32
bf16 = jnp.bfloat16


def dot(a, b):
    return lax.dot_general(a, b, (((1,), (0,)), ((), ())), preferred_element_type=f32)


def head(h):
    return slice(h * HD, (h + 1) * HD)


def expand(slot_values):
    wide = jnp.broadcast_to(slot_values[:, None, :], (slot_values.shape[0], TILE, HD))
    return wide.reshape(slot_values.shape[0] * TILE, HD)


def owner_matrix(plan_ref, slot_ref, device):
    for b in range(PEERS):
        slot_ref[b * SECTIONS : (b + 1) * SECTIONS, :] = plan_ref[b].astype(f32)
    pick = (lax.broadcasted_iota(jnp.int32, (PEERS, HD), 0) == device).astype(bf16)
    tiles = dot(slot_ref[...].astype(bf16), pick)
    column = lax.broadcasted_iota(jnp.int32, (KEYS, HD), 1)
    row = lax.broadcasted_iota(jnp.int32, (KEYS, HD), 0)
    wanted = jnp.where(
        (column & (TILE - 1)) == (row & (TILE - 1)), (column >> 3).astype(f32), -2.0
    )
    return jnp.where(expand(tiles) == wanted, 1.0, 0.0).astype(bf16)


def send_kernel(plan_ref, key_ref, value_ref, out_ref, slot_ref):
    matrix = owner_matrix(plan_ref, slot_ref, lax.axis_index("ctx"))
    out_ref[:, :HD] = dot(matrix, key_ref[...]).astype(bf16)
    out_ref[:, HD:] = dot(matrix, value_ref[...]).astype(bf16)


def row_gate(logit_ref):
    return jax.nn.sigmoid(logit_ref[...])


def causal_scores(key_ref, query_t):
    scores = dot(key_ref[...], query_t)
    key_at = lax.broadcasted_iota(jnp.int32, (ROWS, WIDE), 0)
    row_at = lax.broadcasted_iota(jnp.int32, (ROWS, WIDE), 1) & (ROWS - 1)
    return jnp.where(row_at >= key_at, scores, HIDDEN)


def local_kernel(
    plan_ref, kind_ref, query_ref, key_ref, value_ref, grad_ref, logit_ref,
    query_t_ref, query_s_ref, d_att_t_ref, bias_ref, start_ref, out_t_ref, slot_ref,
):
    gate = row_gate(logit_ref)
    for h in range(GROUP):
        block = query_ref[:, head(h)]
        query_s_ref[head(h), :] = block
        query_t_ref[:, head(h)] = block.astype(f32).T.astype(bf16)
        grad_t = grad_ref[:, head(h)].astype(f32).T
        d_att_t_ref[:, head(h)] = (gate * grad_t).astype(bf16)
    plan = plan_ref[lax.axis_index("ctx")]
    seen = jnp.where(plan >= 0, jnp.where(kind_ref[0] == 0, 2.0, 1.0), 0.0)
    lane = lax.broadcasted_iota(jnp.int32, (SECTIONS, PEERS), 1)
    for p in range(PEERS):
        slot_ref[p * SECTIONS : (p + 1) * SECTIONS, :] = jnp.where(lane == p, seen, 0.0)
    code = dot(slot_ref[...].astype(bf16), jnp.ones((PEERS, HD), bf16))
    need = jnp.where(lax.broadcasted_iota(jnp.int32, (SLOTS, HD), 1) >= ROWS // 2, 0.5, 1.5)
    bias_ref[...] = expand(jnp.where(code > need, 0.0, HIDDEN))
    scores = causal_scores(key_ref, query_t_ref[...])
    top = jnp.max(scores, axis=0, keepdims=True)
    weights = jnp.exp2((scores - top) * SCALE)
    start_ref[0:1, :] = top
    start_ref[1:2, :] = jnp.sum(weights, axis=0, keepdims=True)
    value_t = value_ref[...].astype(f32).T.astype(bf16)
    out_t_ref[...] = dot(value_t, weights.astype(bf16))


def main_kernel(
    kv_ref, query_t_ref, query_s_ref, d_att_t_ref, bias_ref, start_ref, out_t_ref,
    grad_ref, att_t_ref, stat_ref, score_ref, weight_ref,
):
    top = jnp.broadcast_to(start_ref[0:1, :], (TILE, WIDE))
    for c in range(N_CHUNK):
        rows = slice(c * CHUNK, (c + 1) * CHUNK)
        scores = dot(kv_ref[rows, :HD], query_t_ref[...])
        bias = bias_ref[rows, :]
        scores = scores + jnp.concatenate([bias] * GROUP, axis=1)
        score_ref[rows, :] = scores
        top = jnp.maximum(top, jnp.max(scores.reshape(CHUNK // TILE, TILE, WIDE), axis=0))
    top = jnp.max(top, axis=0, keepdims=True)
    total = jnp.zeros((TILE, WIDE), f32)
    out_t = jnp.zeros((HD, WIDE), f32)
    for c in range(N_CHUNK):
        rows = slice(c * CHUNK, (c + 1) * CHUNK)
        weights = jnp.exp2((score_ref[rows, :] - top) * SCALE)
        total = total + jnp.sum(weights.reshape(CHUNK // TILE, TILE, WIDE), axis=0)
        low = weights.astype(bf16)
        weight_ref[rows, :] = low
        out_t = out_t + dot(kv_ref[rows, HD:].T, low)
    share = jnp.exp2((start_ref[0:1, :] - top) * SCALE)
    total = jnp.sum(total, axis=0, keepdims=True) + share * start_ref[1:2, :]
    inverse = 1.0 / total
    att_t = ((out_t + share * out_t_ref[...]) * inverse).astype(bf16)
    att_t_ref[...] = att_t
    d_att_t = d_att_t_ref[...].astype(f32)
    delta = jnp.sum(d_att_t * att_t.astype(f32), axis=0, keepdims=True) * inverse
    d_low_t = (d_att_t * inverse).astype(bf16)
    d_low_s = jnp.concatenate([d_low_t[:, head(h)].T for h in range(GROUP)], axis=0)
    stat_ref[0:1, :] = top
    stat_ref[1:2, :] = inverse
    stat_ref[2:3, :] = delta
    for c in range(N_CHUNK):
        rows = slice(c * CHUNK, (c + 1) * CHUNK)
        low = weight_ref[rows, :]
        grad_ref[rows, HD:] = dot(low, d_low_s).astype(bf16)
        d_probs = dot(kv_ref[rows, HD:], d_low_t)
        d_scores = (low.astype(f32) * (d_probs - delta)).astype(bf16)
        grad_ref[rows, :HD] = (dot(d_scores, query_s_ref[...]) * FACTOR).astype(bf16)


def query_kernel(
    plan_ref, kv_ref, key_ref, value_ref, grad_ref, query_t_ref, query_s_ref, d_att_t_ref, bias_ref,
    att_t_ref, stat_ref, query_grad_ref, local_ref, gate_ref, owner_ref, slot_ref,
):
    top, inverse, delta = stat_ref[0:1, :], stat_ref[1:2, :], stat_ref[2:3, :]
    d_low_t = (d_att_t_ref[...].astype(f32) * inverse).astype(bf16)
    d_low_s = jnp.concatenate([d_low_t[:, head(h)].T for h in range(GROUP)], axis=0)

    def d_score(scores, values):
        weights = jnp.exp2((scores - top) * SCALE)
        d_scores = (weights * (dot(values, d_low_t) - delta)).astype(bf16)
        return weights.astype(bf16), d_scores

    weights, d_scores = d_score(causal_scores(key_ref, query_t_ref[...]), value_ref[...])
    local_ref[:, :HD] = dot(d_scores, query_s_ref[...]) * FACTOR
    local_ref[:, HD:] = dot(weights, d_low_s)
    total = dot(key_ref[...].T, d_scores)
    for c in range(N_CHUNK):
        rows = slice(c * CHUNK, (c + 1) * CHUNK)
        keys = kv_ref[rows, :HD]
        scores = dot(keys, query_t_ref[...]) + jnp.concatenate([bias_ref[rows, :]] * GROUP, axis=1)
        _, d_scores = d_score(scores, kv_ref[rows, HD:])
        total = total + dot(keys.T, d_scores)
    part = jnp.zeros((1, ROWS), f32)
    for h in range(GROUP):
        query_grad_ref[:, head(h)] = (total[:, head(h)] * FACTOR).T.astype(bf16)
        grad_t = grad_ref[:, head(h)].astype(f32).T
        part = part + jnp.sum(grad_t * att_t_ref[:, head(h)].astype(f32), axis=0, keepdims=True)
    gate_ref[...] = part
    matrix = owner_matrix(plan_ref, slot_ref, lax.axis_index("ctx"))
    for c in range(KEYS // HD):
        owner_ref[:, c * HD : (c + 1) * HD] = matrix[c * HD : (c + 1) * HD, :].T


def owner_kernel(owner_ref, returned_ref, local_ref, key_grad_ref, value_grad_ref):
    total = local_ref[...] + dot(owner_ref[...], returned_ref[...])
    key_grad_ref[...] = total[:, :HD].astype(bf16)
    value_grad_ref[...] = total[:, HD:].astype(bf16)


def call(kernel, outs, scratch, flops, moved, *args):
    return pl.pallas_call(
        kernel,
        out_shape=[jax.ShapeDtypeStruct(shape, kind) for shape, kind in outs],
        in_specs=[pl.BlockSpec(memory_space=pltpu.VMEM)] * len(args),
        out_specs=[pl.BlockSpec(memory_space=pltpu.VMEM)] * len(outs),
        scratch_shapes=[pltpu.VMEM(shape, kind) for shape, kind in scratch],
        compiler_params=pltpu.CompilerParams(vmem_limit_bytes=VMEM_LIMIT),
        cost_estimate=pl.CostEstimate(flops=flops, bytes_accessed=moved, transcendentals=0),
        interpret=INTERPRET,
        name=kernel.__name__,
    )(*args)


def exchange(rows):
    pieces = rows.reshape(PEERS, SECTIONS, TILE, 2 * HD)
    moved = lax.all_to_all(pieces, "ctx", split_axis=0, concat_axis=0, tiled=True)
    return moved.reshape(KEYS, 2 * HD)


def body(queries, key_rows, value_rows, out_grad, gate_logit, tile_plan, mask_kind):
    logit = gate_logit.reshape(1, ROWS)
    slot_scratch = ((SLOTS, PEERS), f32)
    (outgoing,) = call(
        send_kernel, [((KEYS, 2 * HD), bf16)], [slot_scratch], 2**27, 2**21,
        tile_plan, key_rows, value_rows,
    )
    fetched = exchange(outgoing)
    query_t, query_s, d_att_t, bias, start, out_t = call(
        local_kernel,
        [((HD, WIDE), bf16), ((WIDE, HD), bf16), ((HD, WIDE), bf16), ((KEYS, HD), f32),
         ((8, WIDE), f32), ((HD, WIDE), f32)],
        [slot_scratch], 2**27, 2**22,
        tile_plan, mask_kind, queries, key_rows, value_rows, out_grad, logit,
    )
    grads, att_t, stat = call(
        main_kernel,
        [((KEYS, 2 * HD), bf16), ((HD, WIDE), bf16), ((8, WIDE), f32)],
        [((KEYS, WIDE), f32), ((KEYS, WIDE), bf16)], 2**31, 2**22,
        fetched, query_t, query_s, d_att_t, bias, start, out_t,
    )
    returned = exchange(grads)
    query_grad, local, gate_part, owner = call(
        query_kernel,
        [((ROWS, WIDE), bf16), ((ROWS, 2 * HD), f32), ((1, ROWS), f32), ((HD, KEYS), bf16)],
        [slot_scratch], 2**31, 2**22,
        tile_plan, fetched, key_rows, value_rows, out_grad, query_t, query_s, d_att_t, bias, att_t, stat,
    )
    gate = jax.nn.sigmoid(gate_logit)
    gate_sum = lax.all_gather(gate_part[0], "head").sum(0)
    gate_grad = gate * (1.0 - gate) * gate_sum
    key_grad, value_grad = call(
        owner_kernel, [((ROWS, HD), bf16), ((ROWS, HD), bf16)], [], 2**27, 2**21,
        owner, returned, local,
    )
    return (query_grad, key_grad, value_grad, gate_grad)


def solution(mesh):
    placed = (
        P("ctx", "head"),
        P("ctx", "head"),
        P("ctx", "head"),
        P("ctx", "head"),
        P("ctx"),
        P(),
        P("ctx", None, None),
    )
    return jax.shard_map(
        body,
        mesh=mesh,
        in_specs=placed,
        out_specs=(P("ctx", "head"), P("ctx", "head"), P("ctx", "head"), P("ctx")),
        check_vma=False,
    )
```

```python
import math

import jax
import jax.numpy as jnp
from jax import lax
from jax.experimental import pallas as pl
from jax.experimental.pallas import tpu as pltpu
from jax.sharding import PartitionSpec as P

HD = 128
TILE = 8
SECTIONS = 4
ROWS = 128
PEERS = 64
GROUP = 6
SLOTS = PEERS * SECTIONS
KEYS = SLOTS * TILE
PICKS = 32
KEPT = SECTIONS * PICKS
NEAR = KEPT * TILE
WIDE = GROUP * ROWS
CHUNK = 256
N_CHUNK = NEAR // CHUNK
SEND_PARTS = 4
FACTOR = 1.0 / math.sqrt(HD)
SCALE = FACTOR * math.log2(math.e)
HIDDEN = -1e30
INTERPRET = False
VMEM_LIMIT = 16 * 1024 * 1024

f32 = jnp.float32
bf16 = jnp.bfloat16


def dot(a, b):
    return lax.dot_general(a, b, (((1,), (0,)), ((), ())), preferred_element_type=f32)


def head(h):
    return slice(h * HD, (h + 1) * HD)


def owner_tiles(plan_ref, slot_ref, device):
    for b in range(PEERS):
        slot_ref[b * SECTIONS : (b + 1) * SECTIONS, :] = plan_ref[b].astype(f32)
    pick = (lax.broadcasted_iota(jnp.int32, (PEERS, HD), 0) == device).astype(bf16)
    return dot(slot_ref[...].astype(bf16), pick)


def owner_matrix(tiles):
    column = lax.broadcasted_iota(jnp.int32, (TILE, HD), 1)
    row = lax.broadcasted_iota(jnp.int32, (TILE, HD), 0)
    wanted = jnp.where((column & (TILE - 1)) == row, (column >> 3).astype(f32), -2.0)
    slots = tiles.shape[0]
    wide = jnp.broadcast_to(tiles[:, None, :], (slots, TILE, HD))
    return jnp.where(wide == wanted[None], 1.0, 0.0).reshape(slots * TILE, HD).astype(bf16)


def send_kernel(plan_hbm, key_hbm, value_hbm, out_hbm, plan_ref, key_ref, value_ref, out_ref, slot_ref, sems):
    loads = [
        pltpu.make_async_copy(plan_hbm, plan_ref, sems.at[0]),
        pltpu.make_async_copy(key_hbm, key_ref, sems.at[1]),
        pltpu.make_async_copy(value_hbm, value_ref, sems.at[2]),
    ]
    for load in loads:
        load.start()
    for load in loads:
        load.wait()
    tiles = owner_tiles(plan_ref, slot_ref, lax.axis_index("ctx"))
    both = jnp.concatenate([key_ref[...], value_ref[...]], axis=1)
    stores = []
    for c in range(SEND_PARTS):
        size = KEYS // SEND_PARTS
        matrix = owner_matrix(tiles[c * size // TILE : (c + 1) * size // TILE])
        out_ref[c * size : (c + 1) * size, :] = dot(matrix, both).astype(bf16)
        part = pl.ds(c * size, size)
        stores.append(pltpu.make_async_copy(out_ref.at[part], out_hbm.at[part], sems.at[3 + c]))
        stores[-1].start()
    for store in stores:
        store.wait()


def row_gate(logit_ref):
    return jax.nn.sigmoid(logit_ref[...])


def causal_scores(key_ref, query_t):
    scores = dot(key_ref[...], query_t)
    key_at = lax.broadcasted_iota(jnp.int32, (ROWS, WIDE), 0)
    row_at = lax.broadcasted_iota(jnp.int32, (ROWS, WIDE), 1) & (ROWS - 1)
    return jnp.where(row_at >= key_at, scores, HIDDEN)


def local_kernel(
    plan_ref, kind_ref, query_ref, key_ref, value_ref, grad_ref, logit_ref,
    query_t_ref, query_s_ref, d_att_t_ref, bias_ref, start_ref, out_t_ref, list_ref,
):
    gate = row_gate(logit_ref)
    for h in range(GROUP):
        block = query_ref[:, head(h)]
        query_s_ref[head(h), :] = block
        query_t_ref[:, head(h)] = block.astype(f32).T.astype(bf16)
        grad_t = grad_ref[:, head(h)].astype(f32).T
        d_att_t_ref[:, head(h)] = (gate * grad_t).astype(bf16)
    scores = causal_scores(key_ref, query_t_ref[...])
    top = jnp.max(scores, axis=0, keepdims=True)
    weights = jnp.exp2((scores - top) * SCALE)
    start_ref[0:1, :] = top
    start_ref[1:2, :] = jnp.sum(weights, axis=0, keepdims=True)
    value_t = value_ref[...].astype(f32).T.astype(bf16)
    out_t_ref[...] = dot(value_t, weights.astype(bf16))
    device = lax.axis_index("ctx")
    bias_ref[...] = jnp.full((NEAR, HD), HIDDEN, f32)
    late = lax.broadcasted_iota(jnp.int32, (TILE, HD), 1) >= ROWS // 2
    for s in range(SECTIONS):

        @pl.loop(0, PICKS)
        def _(k):
            list_ref[s * PICKS + k] = device * SECTIONS + s

        def place(p, count):
            given = plan_ref[s, p] >= 0

            @pl.when(given)
            def _():
                list_ref[s * PICKS + count] = p * SECTIONS + s
                at = pl.multiple_of((s * PICKS + count) * TILE, TILE)
                floor = jnp.where(kind_ref[s, p] == 0, 0.0, HIDDEN)
                bias_ref[pl.ds(at, TILE), :] = jnp.where(late, 0.0, floor)

            return count + given.astype(jnp.int32)

        lax.fori_loop(0, PEERS, place, jnp.int32(0))


def gather_tiles(list_ref, slots_ref, near_ref):
    for k in range(KEPT):
        near_ref[k * TILE : (k + 1) * TILE, :] = slots_ref[list_ref[k]]


def main_kernel(
    list_ref, slots_ref, query_t_ref, bias_ref, start_ref, query_s_hbm, d_att_t_hbm, out_t_hbm,
    grad_hbm, att_t_hbm, stat_hbm,
    kv_ref, grad_ref, score_ref, weight_ref, query_s_ref, d_att_t_ref, out_t_ref, att_t_ref, stat_ref, sems,
):
    loads = [
        pltpu.make_async_copy(query_s_hbm, query_s_ref, sems.at[0]),
        pltpu.make_async_copy(d_att_t_hbm, d_att_t_ref, sems.at[1]),
        pltpu.make_async_copy(out_t_hbm, out_t_ref, sems.at[2]),
    ]
    for load in loads:
        load.start()
    gather_tiles(list_ref, slots_ref, kv_ref)
    grad_ref[...] = jnp.zeros_like(grad_ref)
    top = jnp.broadcast_to(start_ref[0:1, :], (TILE, WIDE))
    for c in range(N_CHUNK):
        rows = slice(c * CHUNK, (c + 1) * CHUNK)
        scores = dot(kv_ref[rows, :HD], query_t_ref[...])
        scores = scores + jnp.concatenate([bias_ref[rows, :]] * GROUP, axis=1)
        score_ref[rows, :] = scores
        top = jnp.maximum(top, jnp.max(scores.reshape(CHUNK // TILE, TILE, WIDE), axis=0))
    top = jnp.max(top, axis=0, keepdims=True)
    total = jnp.zeros((TILE, WIDE), f32)
    out_t = jnp.zeros((HD, WIDE), f32)
    for c in range(N_CHUNK):
        rows = slice(c * CHUNK, (c + 1) * CHUNK)
        weights = jnp.exp2((score_ref[rows, :] - top) * SCALE)
        total = total + jnp.sum(weights.reshape(CHUNK // TILE, TILE, WIDE), axis=0)
        low = weights.astype(bf16)
        weight_ref[rows, :] = low
        out_t = out_t + dot(kv_ref[rows, HD:].T, low)
    share = jnp.exp2((start_ref[0:1, :] - top) * SCALE)
    total = jnp.sum(total, axis=0, keepdims=True) + share * start_ref[1:2, :]
    inverse = 1.0 / total
    for load in loads:
        load.wait()
    att_t = ((out_t + share * out_t_ref[...]) * inverse).astype(bf16)
    att_t_ref[...] = att_t
    d_att_t = d_att_t_ref[...].astype(f32)
    delta = jnp.sum(d_att_t * att_t.astype(f32), axis=0, keepdims=True) * inverse
    d_low_t = (d_att_t * inverse).astype(bf16)
    d_low_s = jnp.concatenate([d_low_t[:, head(h)].T for h in range(GROUP)], axis=0)
    stat_ref[0:1, :] = top
    stat_ref[1:2, :] = inverse
    stat_ref[2:3, :] = delta
    stores = [
        pltpu.make_async_copy(att_t_ref, att_t_hbm, sems.at[3]),
        pltpu.make_async_copy(stat_ref, stat_hbm, sems.at[4]),
    ]

    def scatter(values, c, side):
        for k in range(CHUNK // TILE):
            slot = list_ref[c * (CHUNK // TILE) + k]
            grad_ref[slot, :, side * HD : (side + 1) * HD] = values[k * TILE : (k + 1) * TILE, :]

    def send(side):
        half = pl.ds(side * HD, HD)
        stores.append(
            pltpu.make_async_copy(grad_ref.at[:, :, half], grad_hbm.at[:, :, half], sems.at[5 + side])
        )
        stores[-1].start()

    for store in stores:
        store.start()
    for c in range(N_CHUNK):
        rows = slice(c * CHUNK, (c + 1) * CHUNK)
        scatter(dot(weight_ref[rows, :], d_low_s).astype(bf16), c, 1)
    send(1)
    for c in range(N_CHUNK):
        rows = slice(c * CHUNK, (c + 1) * CHUNK)
        d_probs = dot(kv_ref[rows, HD:], d_low_t)
        d_scores = (weight_ref[rows, :].astype(f32) * (d_probs - delta)).astype(bf16)
        scatter((dot(d_scores, query_s_ref[...]) * FACTOR).astype(bf16), c, 0)
    send(0)
    for store in stores:
        store.wait()


def query_kernel(
    list_ref, plan_ref, slots_ref, key_ref, value_ref, grad_ref, query_t_ref, query_s_ref, d_att_t_ref, bias_ref,
    att_t_ref, stat_ref, query_grad_ref, local_ref, gate_ref, owner_ref, slot_ref, kv_ref,
):
    gather_tiles(list_ref, slots_ref, kv_ref)
    top, inverse, delta = stat_ref[0:1, :], stat_ref[1:2, :], stat_ref[2:3, :]
    d_low_t = (d_att_t_ref[...].astype(f32) * inverse).astype(bf16)
    d_low_s = jnp.concatenate([d_low_t[:, head(h)].T for h in range(GROUP)], axis=0)

    def d_score(scores, values):
        weights = jnp.exp2((scores - top) * SCALE)
        d_scores = (weights * (dot(values, d_low_t) - delta)).astype(bf16)
        return weights.astype(bf16), d_scores

    weights, d_scores = d_score(causal_scores(key_ref, query_t_ref[...]), value_ref[...])
    local_ref[:, :HD] = dot(d_scores, query_s_ref[...]) * FACTOR
    local_ref[:, HD:] = dot(weights, d_low_s)
    total = dot(key_ref[...].T, d_scores)
    for c in range(N_CHUNK):
        rows = slice(c * CHUNK, (c + 1) * CHUNK)
        keys = kv_ref[rows, :HD]
        scores = dot(keys, query_t_ref[...]) + jnp.concatenate([bias_ref[rows, :]] * GROUP, axis=1)
        _, d_scores = d_score(scores, kv_ref[rows, HD:])
        total = total + dot(keys.T, d_scores)
    part = jnp.zeros((1, ROWS), f32)
    for h in range(GROUP):
        query_grad_ref[:, head(h)] = (total[:, head(h)] * FACTOR).T.astype(bf16)
        grad_t = grad_ref[:, head(h)].astype(f32).T
        part = part + jnp.sum(grad_t * att_t_ref[:, head(h)].astype(f32), axis=0, keepdims=True)
    gate_ref[...] = part
    matrix = owner_matrix(owner_tiles(plan_ref, slot_ref, lax.axis_index("ctx")))
    for c in range(KEYS // HD):
        owner_ref[:, c * HD : (c + 1) * HD] = matrix[c * HD : (c + 1) * HD, :].T


def owner_kernel(owner_ref, returned_ref, local_ref, key_grad_ref, value_grad_ref):
    total = local_ref[...] + dot(owner_ref[...], returned_ref[...])
    key_grad_ref[...] = total[:, :HD].astype(bf16)
    value_grad_ref[...] = total[:, HD:].astype(bf16)


VMEM = pltpu.VMEM
SMEM = pltpu.SMEM
HBM = pltpu.HBM


def call(kernel, ins, outs, scratch, flops, moved, limit=VMEM_LIMIT):
    return pl.pallas_call(
        kernel,
        out_shape=[jax.ShapeDtypeStruct(shape, kind) for _, shape, kind in outs],
        in_specs=[pl.BlockSpec(memory_space=space) for space, _ in ins],
        out_specs=[pl.BlockSpec(memory_space=space) for space, _, _ in outs],
        scratch_shapes=scratch,
        compiler_params=pltpu.CompilerParams(vmem_limit_bytes=limit),
        cost_estimate=pl.CostEstimate(flops=flops, bytes_accessed=moved, transcendentals=0),
        interpret=INTERPRET,
        name=kernel.__name__,
    )(*[array for _, array in ins])


def exchange(pieces):
    return lax.all_to_all(pieces, "ctx", split_axis=0, concat_axis=0, tiled=True)


def body(queries, key_rows, value_rows, out_grad, gate_logit, tile_plan, mask_kind):
    logit = gate_logit.reshape(1, ROWS)
    plan_row = lax.dynamic_index_in_dim(tile_plan, lax.axis_index("ctx"), 0, keepdims=False)
    (outgoing,) = call(
        send_kernel,
        [(HBM, tile_plan), (HBM, key_rows), (HBM, value_rows)],
        [(HBM, (KEYS, 2 * HD), bf16)],
        [VMEM((PEERS, SECTIONS, PEERS), jnp.int32), VMEM((ROWS, HD), bf16), VMEM((ROWS, HD), bf16),
         VMEM((KEYS, 2 * HD), bf16),
         VMEM((SLOTS, PEERS), f32), pltpu.SemaphoreType.DMA((3 + SEND_PARTS,))],
        2**27, 2**21, limit=None,
    )
    fetched = exchange(outgoing.reshape(PEERS, SECTIONS, TILE, 2 * HD)).reshape(SLOTS, TILE, 2 * HD)
    query_t, query_s, d_att_t, bias, start, out_t, places = call(
        local_kernel,
        [(SMEM, plan_row), (SMEM, mask_kind[0]), (VMEM, queries), (VMEM, key_rows), (VMEM, value_rows),
         (VMEM, out_grad), (VMEM, logit)],
        [(VMEM, (HD, WIDE), bf16), (VMEM, (WIDE, HD), bf16), (VMEM, (HD, WIDE), bf16), (VMEM, (NEAR, HD), f32),
         (VMEM, (8, WIDE), f32), (VMEM, (HD, WIDE), f32), (SMEM, (KEPT,), jnp.int32)],
        [], 2**27, 2**22,
    )
    grads, att_t, stat = call(
        main_kernel,
        [(SMEM, places), (VMEM, fetched), (VMEM, query_t), (VMEM, bias), (VMEM, start),
         (HBM, query_s), (HBM, d_att_t), (HBM, out_t)],
        [(HBM, (SLOTS, TILE, 2 * HD), bf16), (HBM, (HD, WIDE), bf16), (HBM, (8, WIDE), f32)],
        [VMEM((NEAR, 2 * HD), bf16), VMEM((SLOTS, TILE, 2 * HD), bf16), VMEM((NEAR, WIDE), f32), VMEM((NEAR, WIDE), bf16),
         VMEM((WIDE, HD), bf16), VMEM((HD, WIDE), bf16), VMEM((HD, WIDE), f32), VMEM((HD, WIDE), bf16),
         VMEM((8, WIDE), f32), pltpu.SemaphoreType.DMA((7,))],
        2**30, 2**22,
    )
    returned = exchange(grads.reshape(PEERS, SECTIONS, TILE, 2 * HD)).reshape(KEYS, 2 * HD)
    query_grad, local, gate_part, owner = call(
        query_kernel,
        [(SMEM, places), (VMEM, tile_plan), (VMEM, fetched), (VMEM, key_rows), (VMEM, value_rows), (VMEM, out_grad),
         (VMEM, query_t), (VMEM, query_s), (VMEM, d_att_t), (VMEM, bias), (VMEM, att_t), (VMEM, stat)],
        [(VMEM, (ROWS, WIDE), bf16), (VMEM, (ROWS, 2 * HD), f32), (VMEM, (1, ROWS), f32), (VMEM, (HD, KEYS), bf16)],
        [VMEM((SLOTS, PEERS), f32), VMEM((NEAR, 2 * HD), bf16)],
        2**30, 2**22,
    )
    gate = jax.nn.sigmoid(gate_logit)
    gate_sum = lax.all_gather(gate_part[0], "head").sum(0)
    gate_grad = gate * (1.0 - gate) * gate_sum
    key_grad, value_grad = call(
        owner_kernel,
        [(VMEM, owner), (VMEM, returned), (VMEM, local)],
        [(VMEM, (ROWS, HD), bf16), (VMEM, (ROWS, HD), bf16)],
        [], 2**27, 2**21,
    )
    return (query_grad, key_grad, value_grad, gate_grad)


def solution(mesh):
    placed = (
        P("ctx", "head"),
        P("ctx", "head"),
        P("ctx", "head"),
        P("ctx", "head"),
        P("ctx"),
        P(),
        P("ctx", None, None),
    )
    return jax.shard_map(
        body,
        mesh=mesh,
        in_specs=placed,
        out_specs=(P("ctx", "head"), P("ctx", "head"), P("ctx", "head"), P("ctx")),
        check_vma=False,
    )
```

```python
import math

import jax
import jax.numpy as jnp
from jax import lax
from jax.experimental import pallas as pl
from jax.experimental.pallas import tpu as pltpu
from jax.sharding import PartitionSpec as P

HD = 128
TILE = 8
SECTIONS = 4
ROWS = 128
PEERS = 64
GROUP = 6
SLOTS = PEERS * SECTIONS
KEYS = SLOTS * TILE
PICKS = 32
KEPT = SECTIONS * PICKS
NEAR = KEPT * TILE
WIDE = GROUP * ROWS
CHUNK = 256
PART = 256
N_CHUNK = NEAR // CHUNK
N_PART = WIDE // PART
SEND_PARTS = 4
FACTOR = 1.0 / math.sqrt(HD)
SCALE = FACTOR * math.log2(math.e)
HIDDEN = -1e30
INTERPRET = False
OWNER_LIMIT = 8 * 2**20
MAIN_LIMIT = 16 * 2**20

f32 = jnp.float32
bf16 = jnp.bfloat16


def dot(a, b):
    return lax.dot_general(a, b, (((1,), (0,)), ((), ())), preferred_element_type=f32)


def head(h):
    return slice(h * HD, (h + 1) * HD)


def owner_tiles(plan_ref, slot_ref, device):
    for b in range(PEERS):
        slot_ref[b * SECTIONS : (b + 1) * SECTIONS, :] = plan_ref[b].astype(f32)
    pick = (lax.broadcasted_iota(jnp.int32, (PEERS, HD), 0) == device).astype(bf16)
    return dot(slot_ref[...].astype(bf16), pick)


def owner_matrix(tiles):
    column = lax.broadcasted_iota(jnp.int32, (TILE, HD), 1)
    row = lax.broadcasted_iota(jnp.int32, (TILE, HD), 0)
    wanted = jnp.where((column & (TILE - 1)) == row, (column >> 3).astype(f32), -2.0)
    slots = tiles.shape[0]
    wide = jnp.broadcast_to(tiles[:, None, :], (slots, TILE, HD))
    return jnp.where(wide == wanted[None], 1.0, 0.0).reshape(slots * TILE, HD).astype(bf16)


def send_kernel(plan_hbm, key_hbm, value_hbm, out_hbm, plan_ref, key_ref, value_ref, out_ref, slot_ref, sems):
    loads = [
        pltpu.make_async_copy(plan_hbm, plan_ref, sems.at[0]),
        pltpu.make_async_copy(key_hbm, key_ref, sems.at[1]),
        pltpu.make_async_copy(value_hbm, value_ref, sems.at[2]),
    ]
    for load in loads:
        load.start()
    for load in loads:
        load.wait()
    tiles = owner_tiles(plan_ref, slot_ref, lax.axis_index("ctx"))
    both = jnp.concatenate([key_ref[...], value_ref[...]], axis=1)
    stores = []
    for c in range(SEND_PARTS):
        size = KEYS // SEND_PARTS
        matrix = owner_matrix(tiles[c * size // TILE : (c + 1) * size // TILE])
        out_ref[c * size : (c + 1) * size, :] = dot(matrix, both).astype(bf16)
        part = pl.ds(c * size, size)
        stores.append(pltpu.make_async_copy(out_ref.at[part], out_hbm.at[part], sems.at[3 + c]))
        stores[-1].start()
    for store in stores:
        store.wait()


def row_gate(logit_ref):
    return jax.nn.sigmoid(logit_ref[...])


def causal_scores(key_ref, query_t):
    scores = dot(key_ref[...], query_t)
    key_at = lax.broadcasted_iota(jnp.int32, (ROWS, WIDE), 0)
    row_at = lax.broadcasted_iota(jnp.int32, (ROWS, WIDE), 1) & (ROWS - 1)
    return jnp.where(row_at >= key_at, scores, HIDDEN)


def local_kernel(
    plan_ref, kind_ref, query_ref, key_ref, value_ref, grad_ref, logit_ref,
    query_t_ref, query_s_ref, d_att_t_ref, flag_ref, start_ref, out_t_ref, list_ref,
):
    gate = row_gate(logit_ref)
    for h in range(GROUP):
        block = query_ref[:, head(h)]
        query_s_ref[head(h), :] = block
        query_t_ref[:HD, head(h)] = block.astype(f32).T.astype(bf16)
        grad_t = grad_ref[:, head(h)].astype(f32).T
        d_att_t_ref[:, head(h)] = (gate * grad_t).astype(bf16)
    scores = causal_scores(key_ref, query_t_ref[:HD, :])
    top = jnp.max(scores, axis=0, keepdims=True)
    weights = jnp.exp2((scores - top) * SCALE)
    start_ref[0:1, :] = top
    start_ref[1:2, :] = jnp.sum(weights, axis=0, keepdims=True)
    value_t = value_ref[...].astype(f32).T.astype(bf16)
    out_t_ref[...] = dot(value_t, weights.astype(bf16))
    device = lax.axis_index("ctx")
    flag = lax.broadcasted_iota(jnp.int32, (HD, WIDE), 0)
    early = (lax.broadcasted_iota(jnp.int32, (HD, WIDE), 1) & (ROWS - 1)) < ROWS // 2
    query_t_ref[HD:, :] = jnp.where((flag == 0) | ((flag == 1) & early), HIDDEN, 0.0).astype(bf16)
    lane = lax.broadcasted_iota(jnp.int32, (TILE, HD), 1)
    flag_ref[...] = (lax.broadcasted_iota(jnp.int32, (NEAR, HD), 1) == 0).astype(bf16)
    for s in range(SECTIONS):

        @pl.loop(0, PICKS)
        def _(k):
            list_ref[s * PICKS + k] = device * SECTIONS + s

        def place(p, count):
            given = plan_ref[s, p] >= 0

            @pl.when(given)
            def _():
                list_ref[s * PICKS + count] = p * SECTIONS + s
                at = pl.multiple_of((s * PICKS + count) * TILE, TILE)
                chosen = jnp.where(kind_ref[s, p] == 0, -1, 1)
                flag_ref[pl.ds(at, TILE), :] = (lane == chosen).astype(bf16)

            return count + given.astype(jnp.int32)

        lax.fori_loop(0, PEERS, place, jnp.int32(0))


def main_kernel(
    slots_ref, list_hbm, query_t_hbm, flag_hbm, start_hbm, query_s_hbm, d_att_t_hbm, out_t_hbm,
    grad_hbm, att_t_hbm, stat_hbm, kv_hbm,
    list_ref, query_t_ref, flag_ref, start_ref, query_s_ref, d_att_t_ref, out_t_ref,
    grad_ref, att_t_ref, stat_ref, kv_ref, score_ref, weight_ref, d_score_ref, d_low_ref, sems,
):
    sources = (list_hbm, query_t_hbm, flag_hbm, start_hbm, query_s_hbm, d_att_t_hbm, out_t_hbm)
    places = (list_ref, query_t_ref, flag_ref, start_ref, query_s_ref, d_att_t_ref, out_t_ref)
    loads = [
        pltpu.make_async_copy(source, place, sems.at[n])
        for n, (source, place) in enumerate(zip(sources, places, strict=True))
    ]
    for load in loads:
        load.start()
    grad_ref[...] = jnp.zeros_like(grad_ref)
    for load in loads:
        load.wait()
    for k in range(KEPT):
        kv_ref[k * TILE : (k + 1) * TILE, :] = slots_ref[list_ref[k]]
    value_t = kv_ref[:, HD:].T
    chunks = [slice(c * CHUNK, (c + 1) * CHUNK) for c in range(N_CHUNK)]
    parts = [slice(n * PART, (n + 1) * PART) for n in range(N_PART)]
    tops, totals, outs, deltas, lows = [], [], [], [], []

    def score(n):
        top = jnp.broadcast_to(start_ref[0:1, parts[n]], (TILE, PART))
        for rows in chunks:
            keys = jnp.concatenate([kv_ref[rows, :HD], flag_ref[rows, :]], axis=1)
            scores = dot(keys, query_t_ref[:, parts[n]])
            score_ref[rows, parts[n]] = scores
            top = jnp.maximum(top, jnp.max(scores.reshape(CHUNK // TILE, TILE, PART), axis=0))
        tops.append(jnp.max(top, axis=0, keepdims=True))

    def weigh(n):
        total = jnp.zeros((TILE, PART), f32)
        for rows in chunks:
            weights = jnp.exp2((score_ref[rows, parts[n]] - tops[n]) * SCALE)
            total = total + jnp.sum(weights.reshape(CHUNK // TILE, TILE, PART), axis=0)
            weight_ref[rows, parts[n]] = weights.astype(bf16)
        totals.append(jnp.sum(total, axis=0, keepdims=True))
        outs.append(dot(value_t, weight_ref[:, parts[n]]))

    def finish(n):
        share = jnp.exp2((start_ref[0:1, parts[n]] - tops[n]) * SCALE)
        inverse = 1.0 / (totals[n] + share * start_ref[1:2, parts[n]])
        att_t = ((outs[n] + share * out_t_ref[:, parts[n]]) * inverse).astype(bf16)
        att_t_ref[:, parts[n]] = att_t
        d_att_t = d_att_t_ref[:, parts[n]].astype(f32)
        deltas.append(jnp.sum(d_att_t * att_t.astype(f32), axis=0, keepdims=True) * inverse)
        lows.append((d_att_t * inverse).astype(bf16))
        for h in range(PART // HD):
            at = n * PART + h * HD
            d_low_ref[at : at + HD, :] = lows[n][:, head(h)].T
        stat_ref[0:1, parts[n]] = tops[n]
        stat_ref[1:2, parts[n]] = inverse
        stat_ref[2:3, parts[n]] = deltas[n]

    def back(n):
        for rows in chunks:
            d_probs = dot(kv_ref[rows, HD:], lows[n])
            weights = weight_ref[rows, parts[n]].astype(f32)
            d_score_ref[rows, parts[n]] = (weights * (d_probs - deltas[n])).astype(bf16)

    score(0)
    for n in range(N_PART):
        if n + 1 < N_PART:
            score(n + 1)
        weigh(n)
        if n > 0:
            back(n - 1)
        finish(n)
    back(N_PART - 1)
    stores = [
        pltpu.make_async_copy(att_t_ref, att_t_hbm, sems.at[8]),
        pltpu.make_async_copy(stat_ref, stat_hbm, sems.at[9]),
        pltpu.make_async_copy(kv_ref, kv_hbm, sems.at[7]),
    ]

    def scatter(values, c, side):
        for k in range(CHUNK // TILE):
            slot = list_ref[c * (CHUNK // TILE) + k]
            grad_ref[slot, :, side * HD : (side + 1) * HD] = values[k * TILE : (k + 1) * TILE, :]

    def send(side):
        half = pl.ds(side * HD, HD)
        stores.append(
            pltpu.make_async_copy(grad_ref.at[:, :, half], grad_hbm.at[:, :, half], sems.at[10 + side])
        )
        stores[-1].start()

    for store in stores:
        store.start()
    for c in range(N_CHUNK):
        scatter(dot(weight_ref[chunks[c], :], d_low_ref[...]).astype(bf16), c, 1)
    send(1)
    for c in range(N_CHUNK):
        scatter((dot(d_score_ref[chunks[c], :], query_s_ref[...]) * FACTOR).astype(bf16), c, 0)
    send(0)
    for store in stores:
        store.wait()


def query_kernel(
    plan_ref, kv_ref, key_ref, value_ref, grad_ref, query_t_ref, query_s_ref, d_att_t_ref, flag_ref,
    att_t_ref, stat_ref, query_grad_ref, local_ref, gate_ref, owner_ref, slot_ref,
):
    top, inverse, delta = stat_ref[0:1, :], stat_ref[1:2, :], stat_ref[2:3, :]
    d_low_t = (d_att_t_ref[...].astype(f32) * inverse).astype(bf16)
    d_low_s = jnp.concatenate([d_low_t[:, head(h)].T for h in range(GROUP)], axis=0)

    def d_score(scores, values):
        weights = jnp.exp2((scores - top) * SCALE)
        d_scores = (weights * (dot(values, d_low_t) - delta)).astype(bf16)
        return weights.astype(bf16), d_scores

    weights, d_scores = d_score(causal_scores(key_ref, query_t_ref[:HD, :]), value_ref[...])
    local_ref[:, :HD] = dot(d_scores, query_s_ref[...]) * FACTOR
    local_ref[:, HD:] = dot(weights, d_low_s)
    total = dot(key_ref[...].T, d_scores)
    for c in range(N_CHUNK):
        rows = slice(c * CHUNK, (c + 1) * CHUNK)
        keys = kv_ref[rows, :HD]
        scores = dot(jnp.concatenate([keys, flag_ref[rows, :]], axis=1), query_t_ref[...])
        _, d_scores = d_score(scores, kv_ref[rows, HD:])
        total = total + dot(keys.T, d_scores)
    part = jnp.zeros((1, ROWS), f32)
    for h in range(GROUP):
        query_grad_ref[:, head(h)] = (total[:, head(h)] * FACTOR).T.astype(bf16)
        grad_t = grad_ref[:, head(h)].astype(f32).T
        part = part + jnp.sum(grad_t * att_t_ref[:, head(h)].astype(f32), axis=0, keepdims=True)
    gate_ref[...] = part
    matrix = owner_matrix(owner_tiles(plan_ref, slot_ref, lax.axis_index("ctx")))
    for c in range(KEYS // HD):
        owner_ref[:, c * HD : (c + 1) * HD] = matrix[c * HD : (c + 1) * HD, :].T


def owner_kernel(owner_ref, returned_ref, local_ref, key_grad_ref, value_grad_ref):
    total = local_ref[...] + dot(owner_ref[...], returned_ref[...])
    key_grad_ref[...] = total[:, :HD].astype(bf16)
    value_grad_ref[...] = total[:, HD:].astype(bf16)


VMEM = pltpu.VMEM
SMEM = pltpu.SMEM
HBM = pltpu.HBM


def call(kernel, ins, outs, scratch, flops, moved, limit=None):
    return pl.pallas_call(
        kernel,
        out_shape=[HBM(shape, kind) if space is HBM else jax.ShapeDtypeStruct(shape, kind) for space, shape, kind in outs],
        in_specs=[pl.BlockSpec(memory_space=space) for space, _ in ins],
        out_specs=[pl.BlockSpec(memory_space=space) for space, _, _ in outs],
        scratch_shapes=scratch,
        compiler_params=pltpu.CompilerParams(vmem_limit_bytes=limit),
        cost_estimate=pl.CostEstimate(flops=flops, bytes_accessed=moved, transcendentals=0),
        interpret=INTERPRET,
        name=kernel.__name__,
    )(*[pltpu.with_memory_space_constraint(array, HBM) if space is HBM else array for space, array in ins])


def exchange(pieces):
    return lax.all_to_all(pieces, "ctx", split_axis=0, concat_axis=0, tiled=True)


def body(queries, key_rows, value_rows, out_grad, gate_logit, tile_plan, mask_kind):
    logit = gate_logit.reshape(1, ROWS)
    plan_row = lax.dynamic_index_in_dim(tile_plan, lax.axis_index("ctx"), 0, keepdims=False)
    (outgoing,) = call(
        send_kernel,
        [(HBM, tile_plan), (HBM, key_rows), (HBM, value_rows)],
        [(HBM, (KEYS, 2 * HD), bf16)],
        [VMEM((PEERS, SECTIONS, PEERS), jnp.int32), VMEM((ROWS, HD), bf16), VMEM((ROWS, HD), bf16),
         VMEM((KEYS, 2 * HD), bf16),
         VMEM((SLOTS, PEERS), f32), pltpu.SemaphoreType.DMA((3 + SEND_PARTS,))],
        2**27, 2**21,
    )
    fetched = exchange(outgoing.reshape(PEERS, SECTIONS, TILE, 2 * HD)).reshape(SLOTS, TILE, 2 * HD)
    query_t, query_s, d_att_t, flags, start, out_t, places = call(
        local_kernel,
        [(SMEM, plan_row), (SMEM, mask_kind[0]), (VMEM, queries), (VMEM, key_rows), (VMEM, value_rows),
         (VMEM, out_grad), (VMEM, logit)],
        [(VMEM, (2 * HD, WIDE), bf16), (VMEM, (WIDE, HD), bf16), (VMEM, (HD, WIDE), bf16), (VMEM, (NEAR, HD), bf16),
         (VMEM, (8, WIDE), f32), (VMEM, (HD, WIDE), f32), (SMEM, (KEPT,), jnp.int32)],
        [], 2**27, 2**22,
    )
    grads, att_t, stat, near = call(
        main_kernel,
        [(VMEM, fetched), (HBM, places), (HBM, query_t), (HBM, flags), (HBM, start), (HBM, query_s), (HBM, d_att_t),
         (HBM, out_t)],
        [(HBM, (SLOTS, TILE, 2 * HD), bf16), (HBM, (HD, WIDE), bf16), (HBM, (8, WIDE), f32), (HBM, (NEAR, 2 * HD), bf16)],
        [SMEM((KEPT,), jnp.int32), VMEM((2 * HD, WIDE), bf16), VMEM((NEAR, HD), bf16),
         VMEM((8, WIDE), f32), VMEM((WIDE, HD), bf16), VMEM((HD, WIDE), bf16), VMEM((HD, WIDE), f32),
         VMEM((SLOTS, TILE, 2 * HD), bf16), VMEM((HD, WIDE), bf16), VMEM((8, WIDE), f32), VMEM((NEAR, 2 * HD), bf16),
         VMEM((NEAR, WIDE), f32), VMEM((NEAR, WIDE), bf16), VMEM((NEAR, WIDE), bf16), VMEM((WIDE, HD), bf16),
         pltpu.SemaphoreType.DMA((12,))],
        2**30, 2**22, limit=MAIN_LIMIT,
    )
    returned = exchange(grads.reshape(PEERS, SECTIONS, TILE, 2 * HD)).reshape(KEYS, 2 * HD)
    query_grad, local, gate_part, owner = call(
        query_kernel,
        [(VMEM, tile_plan), (VMEM, near), (VMEM, key_rows), (VMEM, value_rows), (VMEM, out_grad),
         (VMEM, query_t), (VMEM, query_s), (VMEM, d_att_t), (VMEM, flags), (VMEM, att_t), (VMEM, stat)],
        [(VMEM, (ROWS, WIDE), bf16), (VMEM, (ROWS, 2 * HD), f32), (VMEM, (1, ROWS), f32), (VMEM, (HD, KEYS), bf16)],
        [VMEM((SLOTS, PEERS), f32)],
        2**30, 2**22,
    )
    gate = jax.nn.sigmoid(gate_logit)
    gate_sum = lax.all_gather(gate_part[0], "head").sum(0)
    gate_grad = gate * (1.0 - gate) * gate_sum
    key_grad, value_grad = call(
        owner_kernel,
        [(VMEM, owner), (VMEM, returned), (VMEM, local)],
        [(VMEM, (ROWS, HD), bf16), (VMEM, (ROWS, HD), bf16)],
        [], 2**27, 2**21, limit=OWNER_LIMIT,
    )
    return (query_grad, key_grad, value_grad, gate_grad)


def solution(mesh):
    placed = (
        P("ctx", "head"),
        P("ctx", "head"),
        P("ctx", "head"),
        P("ctx", "head"),
        P("ctx"),
        P(),
        P("ctx", None, None),
    )
    return jax.shard_map(
        body,
        mesh=mesh,
        in_specs=placed,
        out_specs=(P("ctx", "head"), P("ctx", "head"), P("ctx", "head"), P("ctx")),
        check_vma=False,
    )
```

```python
import math

import jax
import jax.numpy as jnp
from jax import lax
from jax.experimental import pallas as pl
from jax.experimental.pallas import tpu as pltpu
from jax.sharding import PartitionSpec as P

HD = 128
TILE = 8
SECTIONS = 4
ROWS = 128
PEERS = 64
GROUP = 6
SLOTS = PEERS * SECTIONS
KEYS = SLOTS * TILE
PICKS = 32
KEPT = SECTIONS * PICKS
NEAR = KEPT * TILE
WIDE = GROUP * ROWS
CHUNK = 256
PART = 256
N_CHUNK = NEAR // CHUNK
N_PART = WIDE // PART
SEND_PARTS = 4
FACTOR = 1.0 / math.sqrt(HD)
SCALE = FACTOR * math.log2(math.e)
HIDDEN = -1e30
INTERPRET = False
VMEM_LIMIT = 16 * 2**20

f32 = jnp.float32
bf16 = jnp.bfloat16


def dot(a, b):
    return lax.dot_general(a, b, (((1,), (0,)), ((), ())), preferred_element_type=f32)


def head(h):
    return slice(h * HD, (h + 1) * HD)


def owner_tiles(plan_ref, slot_ref, device):
    for b in range(PEERS):
        slot_ref[b * SECTIONS : (b + 1) * SECTIONS, :] = plan_ref[b].astype(f32)
    pick = (lax.broadcasted_iota(jnp.int32, (PEERS, HD), 0) == device).astype(bf16)
    return dot(slot_ref[...].astype(bf16), pick)


def owner_matrix(tiles):
    column = lax.broadcasted_iota(jnp.int32, (TILE, HD), 1)
    row = lax.broadcasted_iota(jnp.int32, (TILE, HD), 0)
    wanted = jnp.where((column & (TILE - 1)) == row, (column >> 3).astype(f32), -2.0)
    slots = tiles.shape[0]
    wide = jnp.broadcast_to(tiles[:, None, :], (slots, TILE, HD))
    return jnp.where(wide == wanted[None], 1.0, 0.0).reshape(slots * TILE, HD).astype(bf16)


def send_kernel(plan_hbm, key_hbm, value_hbm, out_hbm, plan_ref, key_ref, value_ref, out_ref, slot_ref, sems):
    loads = [
        pltpu.make_async_copy(plan_hbm, plan_ref, sems.at[0]),
        pltpu.make_async_copy(key_hbm, key_ref, sems.at[1]),
        pltpu.make_async_copy(value_hbm, value_ref, sems.at[2]),
    ]
    for load in loads:
        load.start()
    for load in loads:
        load.wait()
    tiles = owner_tiles(plan_ref, slot_ref, lax.axis_index("ctx"))
    both = jnp.concatenate([key_ref[...], value_ref[...]], axis=1)
    stores = []
    for c in range(SEND_PARTS):
        size = KEYS // SEND_PARTS
        matrix = owner_matrix(tiles[c * size // TILE : (c + 1) * size // TILE])
        out_ref[c * size : (c + 1) * size, :] = dot(matrix, both).astype(bf16)
        part = pl.ds(c * size, size)
        stores.append(pltpu.make_async_copy(out_ref.at[part], out_hbm.at[part], sems.at[3 + c]))
        stores[-1].start()
    for store in stores:
        store.wait()


def row_gate(logit_ref):
    return jax.nn.sigmoid(logit_ref[...])


def causal_scores(key_ref, query_t):
    scores = dot(key_ref[...], query_t)
    key_at = lax.broadcasted_iota(jnp.int32, (ROWS, WIDE), 0)
    row_at = lax.broadcasted_iota(jnp.int32, (ROWS, WIDE), 1) & (ROWS - 1)
    return jnp.where(row_at >= key_at, scores, HIDDEN)


def local_kernel(
    plan_ref, kind_ref, query_ref, key_ref, value_ref, grad_ref, logit_ref,
    query_t_ref, query_s_ref, d_att_t_ref, flag_ref, start_ref, out_t_ref, list_ref,
    query_t_hbm, query_s_hbm, d_att_t_hbm, flag_hbm, sems,
):
    gate = row_gate(logit_ref)
    for h in range(GROUP):
        block = query_ref[:, head(h)]
        query_s_ref[head(h), :] = block
        query_t_ref[:HD, head(h)] = block.astype(f32).T.astype(bf16)
        grad_t = grad_ref[:, head(h)].astype(f32).T
        d_att_t_ref[:, head(h)] = (gate * grad_t).astype(bf16)
    scores = causal_scores(key_ref, query_t_ref[:HD, :])
    top = jnp.max(scores, axis=0, keepdims=True)
    weights = jnp.exp2((scores - top) * SCALE)
    start_ref[0:1, :] = top
    start_ref[1:2, :] = jnp.sum(weights, axis=0, keepdims=True)
    value_t = value_ref[...].astype(f32).T.astype(bf16)
    out_t_ref[...] = dot(value_t, weights.astype(bf16))
    device = lax.axis_index("ctx")
    flag = lax.broadcasted_iota(jnp.int32, (HD, WIDE), 0)
    early = (lax.broadcasted_iota(jnp.int32, (HD, WIDE), 1) & (ROWS - 1)) < ROWS // 2
    query_t_ref[HD:, :] = jnp.where((flag == 0) | ((flag == 1) & early), HIDDEN, 0.0).astype(bf16)
    lane = lax.broadcasted_iota(jnp.int32, (TILE, HD), 1)
    flag_ref[...] = (lax.broadcasted_iota(jnp.int32, (NEAR, HD), 1) == 0).astype(bf16)
    for s in range(SECTIONS):

        @pl.loop(0, PICKS)
        def _(k):
            list_ref[s * PICKS + k] = device * SECTIONS + s

        def place(p, count):
            given = plan_ref[s, p] >= 0

            @pl.when(given)
            def _():
                list_ref[s * PICKS + count] = p * SECTIONS + s
                at = pl.multiple_of((s * PICKS + count) * TILE, TILE)
                chosen = jnp.where(kind_ref[s, p] == 0, -1, 1)
                flag_ref[pl.ds(at, TILE), :] = (lane == chosen).astype(bf16)

            return count + given.astype(jnp.int32)

        lax.fori_loop(0, PEERS, place, jnp.int32(0))
    sources = (query_t_ref, query_s_ref, d_att_t_ref, flag_ref)
    copies = (query_t_hbm, query_s_hbm, d_att_t_hbm, flag_hbm)
    stores = [
        pltpu.make_async_copy(source, copy, sems.at[n])
        for n, (source, copy) in enumerate(zip(sources, copies, strict=True))
    ]
    for store in stores:
        store.start()
    for store in stores:
        store.wait()


def main_kernel(
    list_ref, slots_ref, query_t_ref, flag_ref, start_ref, query_s_ref, d_att_t_ref, out_t_ref,
    grad_hbm, att_t_hbm, stat_hbm, kv_hbm,
    grad_ref, att_t_ref, stat_ref, kv_ref, score_ref, weight_ref, d_score_ref, d_low_ref, sems,
):
    grad_ref[...] = jnp.zeros_like(grad_ref)
    for k in range(KEPT):
        kv_ref[k * TILE : (k + 1) * TILE, :] = slots_ref[list_ref[k]]
    value_t = kv_ref[:, HD:].T
    chunks = [slice(c * CHUNK, (c + 1) * CHUNK) for c in range(N_CHUNK)]
    parts = [slice(n * PART, (n + 1) * PART) for n in range(N_PART)]
    tops, totals, outs, deltas, lows = [], [], [], [], []

    def score(n):
        top = jnp.broadcast_to(start_ref[0:1, parts[n]], (TILE, PART))
        for rows in chunks:
            keys = jnp.concatenate([kv_ref[rows, :HD], flag_ref[rows, :]], axis=1)
            scores = dot(keys, query_t_ref[:, parts[n]])
            score_ref[rows, parts[n]] = scores
            top = jnp.maximum(top, jnp.max(scores.reshape(CHUNK // TILE, TILE, PART), axis=0))
        tops.append(jnp.max(top, axis=0, keepdims=True))

    def weigh(n):
        total = jnp.zeros((TILE, PART), f32)
        for rows in chunks:
            weights = jnp.exp2((score_ref[rows, parts[n]] - tops[n]) * SCALE)
            total = total + jnp.sum(weights.reshape(CHUNK // TILE, TILE, PART), axis=0)
            weight_ref[rows, parts[n]] = weights.astype(bf16)
        totals.append(jnp.sum(total, axis=0, keepdims=True))
        outs.append(dot(value_t, weight_ref[:, parts[n]]))

    def finish(n):
        share = jnp.exp2((start_ref[0:1, parts[n]] - tops[n]) * SCALE)
        inverse = 1.0 / (totals[n] + share * start_ref[1:2, parts[n]])
        att_t = ((outs[n] + share * out_t_ref[:, parts[n]]) * inverse).astype(bf16)
        att_t_ref[:, parts[n]] = att_t
        d_att_t = d_att_t_ref[:, parts[n]].astype(f32)
        deltas.append(jnp.sum(d_att_t * att_t.astype(f32), axis=0, keepdims=True) * inverse)
        lows.append((d_att_t * inverse).astype(bf16))
        for h in range(PART // HD):
            at = n * PART + h * HD
            d_low_ref[at : at + HD, :] = lows[n][:, head(h)].T
        stat_ref[0:1, parts[n]] = tops[n]
        stat_ref[1:2, parts[n]] = inverse
        stat_ref[2:3, parts[n]] = deltas[n]

    def back(n):
        for rows in chunks:
            d_probs = dot(kv_ref[rows, HD:], lows[n])
            weights = weight_ref[rows, parts[n]].astype(f32)
            d_score_ref[rows, parts[n]] = (weights * (d_probs - deltas[n])).astype(bf16)

    score(0)
    for n in range(N_PART):
        if n + 1 < N_PART:
            score(n + 1)
        weigh(n)
        if n > 0:
            back(n - 1)
        finish(n)
    back(N_PART - 1)
    stores = [
        pltpu.make_async_copy(att_t_ref, att_t_hbm, sems.at[1]),
        pltpu.make_async_copy(stat_ref, stat_hbm, sems.at[2]),
        pltpu.make_async_copy(kv_ref, kv_hbm, sems.at[0]),
    ]

    def scatter(values, c, side):
        for k in range(CHUNK // TILE):
            slot = list_ref[c * (CHUNK // TILE) + k]
            grad_ref[slot, :, side * HD : (side + 1) * HD] = values[k * TILE : (k + 1) * TILE, :]

    def send(side):
        half = pl.ds(side * HD, HD)
        stores.append(
            pltpu.make_async_copy(grad_ref.at[:, :, half], grad_hbm.at[:, :, half], sems.at[3 + side])
        )
        stores[-1].start()

    for store in stores:
        store.start()
    for c in range(N_CHUNK):
        scatter(dot(weight_ref[chunks[c], :], d_low_ref[...]).astype(bf16), c, 1)
    send(1)
    for c in range(N_CHUNK):
        scatter((dot(d_score_ref[chunks[c], :], query_s_ref[...]) * FACTOR).astype(bf16), c, 0)
    send(0)
    for store in stores:
        store.wait()


def query_kernel(
    plan_ref, kv_ref, key_ref, value_ref, grad_ref, query_t_ref, query_s_ref, d_att_t_ref, flag_ref,
    att_t_ref, stat_ref, query_grad_ref, local_ref, gate_ref, owner_ref, slot_ref,
):
    top, inverse, delta = stat_ref[0:1, :], stat_ref[1:2, :], stat_ref[2:3, :]
    d_low_t = (d_att_t_ref[...].astype(f32) * inverse).astype(bf16)
    d_low_s = jnp.concatenate([d_low_t[:, head(h)].T for h in range(GROUP)], axis=0)

    def d_score(scores, values):
        weights = jnp.exp2((scores - top) * SCALE)
        d_scores = (weights * (dot(values, d_low_t) - delta)).astype(bf16)
        return weights.astype(bf16), d_scores

    weights, d_scores = d_score(causal_scores(key_ref, query_t_ref[:HD, :]), value_ref[...])
    local_ref[:, :HD] = dot(d_scores, query_s_ref[...]) * FACTOR
    local_ref[:, HD:] = dot(weights, d_low_s)
    total = dot(key_ref[...].T, d_scores)
    for c in range(N_CHUNK):
        rows = slice(c * CHUNK, (c + 1) * CHUNK)
        keys = kv_ref[rows, :HD]
        scores = dot(jnp.concatenate([keys, flag_ref[rows, :]], axis=1), query_t_ref[...])
        _, d_scores = d_score(scores, kv_ref[rows, HD:])
        total = total + dot(keys.T, d_scores)
    part = jnp.zeros((1, ROWS), f32)
    for h in range(GROUP):
        query_grad_ref[:, head(h)] = (total[:, head(h)] * FACTOR).T.astype(bf16)
        grad_t = grad_ref[:, head(h)].astype(f32).T
        part = part + jnp.sum(grad_t * att_t_ref[:, head(h)].astype(f32), axis=0, keepdims=True)
    gate_ref[...] = part
    matrix = owner_matrix(owner_tiles(plan_ref, slot_ref, lax.axis_index("ctx")))
    for c in range(KEYS // HD):
        owner_ref[:, c * HD : (c + 1) * HD] = matrix[c * HD : (c + 1) * HD, :].T


def owner_kernel(owner_ref, returned_ref, local_ref, key_grad_ref, value_grad_ref):
    total = local_ref[...] + dot(owner_ref[...], returned_ref[...])
    key_grad_ref[...] = total[:, :HD].astype(bf16)
    value_grad_ref[...] = total[:, HD:].astype(bf16)


VMEM = pltpu.VMEM
SMEM = pltpu.SMEM
HBM = pltpu.HBM


def call(kernel, ins, outs, scratch, flops, moved, limit=None):
    return pl.pallas_call(
        kernel,
        out_shape=[HBM(shape, kind) if space is HBM else jax.ShapeDtypeStruct(shape, kind) for space, shape, kind in outs],
        in_specs=[pl.BlockSpec(memory_space=space) for space, _ in ins],
        out_specs=[pl.BlockSpec(memory_space=space) for space, _, _ in outs],
        scratch_shapes=scratch,
        compiler_params=pltpu.CompilerParams(vmem_limit_bytes=limit),
        cost_estimate=pl.CostEstimate(flops=flops, bytes_accessed=moved, transcendentals=0),
        interpret=INTERPRET,
        name=kernel.__name__,
    )(*[pltpu.with_memory_space_constraint(array, HBM) if space is HBM else array for space, array in ins])


def exchange(pieces):
    return lax.all_to_all(pieces, "ctx", split_axis=0, concat_axis=0, tiled=True)


def body(queries, key_rows, value_rows, out_grad, gate_logit, tile_plan, mask_kind):
    logit = gate_logit.reshape(1, ROWS)
    plan_row = lax.dynamic_index_in_dim(tile_plan, lax.axis_index("ctx"), 0, keepdims=False)
    (outgoing,) = call(
        send_kernel,
        [(HBM, tile_plan), (HBM, key_rows), (HBM, value_rows)],
        [(HBM, (KEYS, 2 * HD), bf16)],
        [VMEM((PEERS, SECTIONS, PEERS), jnp.int32), VMEM((ROWS, HD), bf16), VMEM((ROWS, HD), bf16),
         VMEM((KEYS, 2 * HD), bf16),
         VMEM((SLOTS, PEERS), f32), pltpu.SemaphoreType.DMA((3 + SEND_PARTS,))],
        2**27, 2**21,
    )
    fetched = exchange(outgoing.reshape(PEERS, SECTIONS, TILE, 2 * HD)).reshape(SLOTS, TILE, 2 * HD)
    query_t, query_s, d_att_t, flags, start, out_t, places, *again = call(
        local_kernel,
        [(SMEM, plan_row), (SMEM, mask_kind[0]), (VMEM, queries), (VMEM, key_rows), (VMEM, value_rows),
         (VMEM, out_grad), (VMEM, logit)],
        [(VMEM, (2 * HD, WIDE), bf16), (VMEM, (WIDE, HD), bf16), (VMEM, (HD, WIDE), bf16), (VMEM, (NEAR, HD), bf16),
         (VMEM, (8, WIDE), f32), (VMEM, (HD, WIDE), f32), (SMEM, (KEPT,), jnp.int32),
         (HBM, (2 * HD, WIDE), bf16), (HBM, (WIDE, HD), bf16), (HBM, (HD, WIDE), bf16), (HBM, (NEAR, HD), bf16)],
        [pltpu.SemaphoreType.DMA((4,))], 2**27, 2**22, limit=VMEM_LIMIT,
    )
    grads, att_t, stat, near = call(
        main_kernel,
        [(SMEM, places), (VMEM, fetched), (VMEM, query_t), (VMEM, flags), (VMEM, start), (VMEM, query_s), (VMEM, d_att_t),
         (VMEM, out_t)],
        [(HBM, (SLOTS, TILE, 2 * HD), bf16), (HBM, (HD, WIDE), bf16), (HBM, (8, WIDE), f32), (HBM, (NEAR, 2 * HD), bf16)],
        [VMEM((SLOTS, TILE, 2 * HD), bf16), VMEM((HD, WIDE), bf16), VMEM((8, WIDE), f32), VMEM((NEAR, 2 * HD), bf16),
         VMEM((NEAR, WIDE), f32), VMEM((NEAR, WIDE), bf16), VMEM((NEAR, WIDE), bf16), VMEM((WIDE, HD), bf16),
         pltpu.SemaphoreType.DMA((5,))],
        2**30, 2**22, limit=VMEM_LIMIT,
    )
    returned = exchange(grads.reshape(PEERS, SECTIONS, TILE, 2 * HD)).reshape(KEYS, 2 * HD)
    query_grad, local, gate_part, owner = call(
        query_kernel,
        [(VMEM, tile_plan), (VMEM, near), (VMEM, key_rows), (VMEM, value_rows), (VMEM, out_grad),
         *[(VMEM, array) for array in again], (VMEM, att_t), (VMEM, stat)],
        [(VMEM, (ROWS, WIDE), bf16), (VMEM, (ROWS, 2 * HD), f32), (VMEM, (1, ROWS), f32), (VMEM, (HD, KEYS), bf16)],
        [VMEM((SLOTS, PEERS), f32)],
        2**30, 2**22, limit=VMEM_LIMIT,
    )
    gate = jax.nn.sigmoid(gate_logit)
    gate_sum = lax.all_gather(gate_part[0], "head").sum(0)
    gate_grad = gate * (1.0 - gate) * gate_sum
    key_grad, value_grad = call(
        owner_kernel,
        [(VMEM, owner), (VMEM, returned), (VMEM, local)],
        [(VMEM, (ROWS, HD), bf16), (VMEM, (ROWS, HD), bf16)],
        [], 2**27, 2**21, limit=VMEM_LIMIT,
    )
    return (query_grad, key_grad, value_grad, gate_grad)


def solution(mesh):
    placed = (
        P("ctx", "head"),
        P("ctx", "head"),
        P("ctx", "head"),
        P("ctx", "head"),
        P("ctx"),
        P(),
        P("ctx", None, None),
    )
    return jax.shard_map(
        body,
        mesh=mesh,
        in_specs=placed,
        out_specs=(P("ctx", "head"), P("ctx", "head"), P("ctx", "head"), P("ctx")),
        check_vma=False,
    )
```

```python
import math

import jax
import jax.numpy as jnp
from jax import lax
from jax.experimental import pallas as pl
from jax.experimental.pallas import tpu as pltpu
from jax.sharding import PartitionSpec as P

HD = 128
TILE = 8
SECTIONS = 4
ROWS = 128
PEERS = 64
GROUP = 6
SLOTS = PEERS * SECTIONS
KEYS = SLOTS * TILE
PICKS = 32
KEPT = SECTIONS * PICKS
NEAR = KEPT * TILE
WIDE = GROUP * ROWS
CHUNK = 256
PART = 256
N_CHUNK = NEAR // CHUNK
N_PART = WIDE // PART
SEND_PARTS = 4
FACTOR = 1.0 / math.sqrt(HD)
SCALE = FACTOR * math.log2(math.e)
HIDDEN = -1e30
INTERPRET = False
VMEM_LIMIT = 16 * 2**20

f32 = jnp.float32
bf16 = jnp.bfloat16


def dot(a, b):
    return lax.dot_general(a, b, (((1,), (0,)), ((), ())), preferred_element_type=f32)


def head(h):
    return slice(h * HD, (h + 1) * HD)


def owner_tiles(plan_ref, slot_ref, device):
    for b in range(PEERS):
        slot_ref[b * SECTIONS : (b + 1) * SECTIONS, :] = plan_ref[b].astype(f32)
    pick = (lax.broadcasted_iota(jnp.int32, (PEERS, HD), 0) == device).astype(bf16)
    return dot(slot_ref[...].astype(bf16), pick)


def owner_matrix(tiles):
    column = lax.broadcasted_iota(jnp.int32, (TILE, HD), 1)
    row = lax.broadcasted_iota(jnp.int32, (TILE, HD), 0)
    wanted = jnp.where((column & (TILE - 1)) == row, (column >> 3).astype(f32), -2.0)
    slots = tiles.shape[0]
    wide = jnp.broadcast_to(tiles[:, None, :], (slots, TILE, HD))
    return jnp.where(wide == wanted[None], 1.0, 0.0).reshape(slots * TILE, HD).astype(bf16)


def send_kernel(plan_hbm, key_hbm, value_hbm, out_hbm, plan_ref, key_ref, value_ref, out_ref, slot_ref, sems):
    loads = [
        pltpu.make_async_copy(plan_hbm, plan_ref, sems.at[0]),
        pltpu.make_async_copy(key_hbm, key_ref, sems.at[1]),
        pltpu.make_async_copy(value_hbm, value_ref, sems.at[2]),
    ]
    for load in loads:
        load.start()
    for load in loads:
        load.wait()
    tiles = owner_tiles(plan_ref, slot_ref, lax.axis_index("ctx"))
    both = jnp.concatenate([key_ref[...], value_ref[...]], axis=1)
    stores = []
    for c in range(SEND_PARTS):
        size = KEYS // SEND_PARTS
        matrix = owner_matrix(tiles[c * size // TILE : (c + 1) * size // TILE])
        out_ref[c * size : (c + 1) * size, :] = dot(matrix, both).astype(bf16)
        part = pl.ds(c * size, size)
        stores.append(pltpu.make_async_copy(out_ref.at[part], out_hbm.at[part], sems.at[3 + c]))
        stores[-1].start()
    for store in stores:
        store.wait()


def row_gate(logit_ref):
    return jax.nn.sigmoid(logit_ref[...])


def causal_scores(key_ref, query_t):
    scores = dot(key_ref[...], query_t)
    key_at = lax.broadcasted_iota(jnp.int32, (ROWS, WIDE), 0)
    row_at = lax.broadcasted_iota(jnp.int32, (ROWS, WIDE), 1) & (ROWS - 1)
    return jnp.where(row_at >= key_at, scores, HIDDEN)


def local_kernel(
    plan_ref, kind_ref, query_ref, key_ref, value_ref, grad_ref, logit_ref,
    query_t_ref, query_s_ref, d_att_t_ref, flag_ref, start_ref, out_t_ref, list_ref,
    query_t_hbm, query_s_hbm, d_att_t_hbm, flag_hbm, sems,
):
    gate = row_gate(logit_ref)
    for h in range(GROUP):
        block = query_ref[:, head(h)]
        query_s_ref[head(h), :] = block
        query_t_ref[:HD, head(h)] = block.astype(f32).T.astype(bf16)
        grad_t = grad_ref[:, head(h)].astype(f32).T
        d_att_t_ref[:, head(h)] = (gate * grad_t).astype(bf16)
    scores = causal_scores(key_ref, query_t_ref[:HD, :])
    top = jnp.max(scores, axis=0, keepdims=True)
    weights = jnp.exp2((scores - top) * SCALE)
    start_ref[0:1, :] = top
    start_ref[1:2, :] = jnp.sum(weights, axis=0, keepdims=True)
    value_t = value_ref[...].astype(f32).T.astype(bf16)
    out_t_ref[...] = dot(value_t, weights.astype(bf16))
    device = lax.axis_index("ctx")
    flag = lax.broadcasted_iota(jnp.int32, (HD, WIDE), 0)
    early = (lax.broadcasted_iota(jnp.int32, (HD, WIDE), 1) & (ROWS - 1)) < ROWS // 2
    query_t_ref[HD:, :] = jnp.where((flag == 0) | ((flag == 1) & early), HIDDEN, 0.0).astype(bf16)
    lane = lax.broadcasted_iota(jnp.int32, (TILE, HD), 1)
    flag_ref[...] = (lax.broadcasted_iota(jnp.int32, (NEAR, HD), 1) == 0).astype(bf16)
    for s in range(SECTIONS):

        @pl.loop(0, PICKS)
        def _(k):
            list_ref[s * PICKS + k] = device * SECTIONS + s

        def place(p, count):
            given = plan_ref[s, p] >= 0

            @pl.when(given)
            def _():
                list_ref[s * PICKS + count] = p * SECTIONS + s
                at = pl.multiple_of((s * PICKS + count) * TILE, TILE)
                chosen = jnp.where(kind_ref[s, p] == 0, -1, 1)
                flag_ref[pl.ds(at, TILE), :] = (lane == chosen).astype(bf16)

            return count + given.astype(jnp.int32)

        lax.fori_loop(0, PEERS, place, jnp.int32(0))
    sources = (query_t_ref, query_s_ref, d_att_t_ref, flag_ref)
    copies = (query_t_hbm, query_s_hbm, d_att_t_hbm, flag_hbm)
    stores = [
        pltpu.make_async_copy(source, copy, sems.at[n])
        for n, (source, copy) in enumerate(zip(sources, copies, strict=True))
    ]
    for store in stores:
        store.start()
    for store in stores:
        store.wait()


def main_kernel(
    list_in_ref, slots_ref, query_t_ref, flag_ref, start_ref, query_s_ref, d_att_t_ref, out_t_ref,
    grad_hbm, att_t_hbm, stat_hbm, kv_hbm,
    list_ref, grad_ref, att_t_ref, stat_ref, kv_ref, score_ref, weight_ref, d_score_ref, d_low_ref, sems,
):
    load = pltpu.make_async_copy(list_in_ref, list_ref, sems.at[5])
    load.start()
    grad_ref[...] = jnp.zeros_like(grad_ref)
    load.wait()
    for k in range(KEPT):
        kv_ref[k * TILE : (k + 1) * TILE, :] = slots_ref[list_ref[k]]
    value_t = kv_ref[:, HD:].T
    chunks = [slice(c * CHUNK, (c + 1) * CHUNK) for c in range(N_CHUNK)]
    parts = [slice(n * PART, (n + 1) * PART) for n in range(N_PART)]
    tops, totals, outs, deltas, lows = [], [], [], [], []

    def score(n):
        top = jnp.broadcast_to(start_ref[0:1, parts[n]], (TILE, PART))
        for rows in chunks:
            keys = jnp.concatenate([kv_ref[rows, :HD], flag_ref[rows, :]], axis=1)
            scores = dot(keys, query_t_ref[:, parts[n]])
            score_ref[rows, parts[n]] = scores
            top = jnp.maximum(top, jnp.max(scores.reshape(CHUNK // TILE, TILE, PART), axis=0))
        tops.append(jnp.max(top, axis=0, keepdims=True))

    def weigh(n):
        total = jnp.zeros((TILE, PART), f32)
        for c in range(NEAR // 32):
            rows = slice(c * 32, (c + 1) * 32)
            weights = jnp.exp2((score_ref[rows, parts[n]] - tops[n]) * SCALE)
            total = total + jnp.sum(weights.reshape(32 // TILE, TILE, PART), axis=0)
            weight_ref[rows, parts[n]] = weights.astype(bf16)
        totals.append(jnp.sum(total, axis=0, keepdims=True))
        outs.append(dot(value_t, weight_ref[:, parts[n]]))

    def finish(n):
        share = jnp.exp2((start_ref[0:1, parts[n]] - tops[n]) * SCALE)
        inverse = 1.0 / (totals[n] + share * start_ref[1:2, parts[n]])
        att_t = ((outs[n] + share * out_t_ref[:, parts[n]]) * inverse).astype(bf16)
        att_t_ref[:, parts[n]] = att_t
        d_att_t = d_att_t_ref[:, parts[n]].astype(f32)
        deltas.append(jnp.sum(d_att_t * att_t.astype(f32), axis=0, keepdims=True) * inverse)
        lows.append((d_att_t * inverse).astype(bf16))
        for h in range(PART // HD):
            at = n * PART + h * HD
            d_low_ref[at : at + HD, :] = lows[n][:, head(h)].T
        stat_ref[0:1, parts[n]] = tops[n]
        stat_ref[1:2, parts[n]] = inverse
        stat_ref[2:3, parts[n]] = deltas[n]

    def back(n):
        for rows in chunks:
            d_probs = dot(kv_ref[rows, HD:], lows[n])
            weights = weight_ref[rows, parts[n]].astype(f32)
            d_score_ref[rows, parts[n]] = (weights * (d_probs - deltas[n])).astype(bf16)

    score(0)
    for n in range(N_PART):
        if n + 1 < N_PART:
            score(n + 1)
        weigh(n)
        if n > 0:
            back(n - 1)
        finish(n)
    stores = [
        pltpu.make_async_copy(att_t_ref, att_t_hbm, sems.at[1]),
        pltpu.make_async_copy(stat_ref, stat_hbm, sems.at[2]),
        pltpu.make_async_copy(kv_ref, kv_hbm, sems.at[0]),
    ]

    def scatter(values, c, side):
        for k in range(CHUNK // TILE):
            slot = list_ref[c * (CHUNK // TILE) + k]
            grad_ref[slot, :, side * HD : (side + 1) * HD] = values[k * TILE : (k + 1) * TILE, :]

    def send(side):
        half = pl.ds(side * HD, HD)
        stores.append(
            pltpu.make_async_copy(grad_ref.at[:, :, half], grad_hbm.at[:, :, half], sems.at[3 + side])
        )
        stores[-1].start()

    for store in stores:
        store.start()
    for c in range(N_CHUNK):
        scatter(dot(weight_ref[chunks[c], :], d_low_ref[...]).astype(bf16), c, 1)
    send(1)
    back(N_PART - 1)
    for c in range(N_CHUNK):
        scatter((dot(d_score_ref[chunks[c], :], query_s_ref[...]) * FACTOR).astype(bf16), c, 0)
    send(0)
    for store in stores:
        store.wait()


def query_kernel(
    plan_ref, kv_ref, key_ref, value_ref, grad_ref, query_t_ref, query_s_ref, d_att_t_ref, flag_ref,
    att_t_ref, stat_ref, query_grad_ref, local_ref, gate_ref, owner_ref, slot_ref,
):
    top, inverse, delta = stat_ref[0:1, :], stat_ref[1:2, :], stat_ref[2:3, :]
    d_low_t = (d_att_t_ref[...].astype(f32) * inverse).astype(bf16)
    d_low_s = jnp.concatenate([d_low_t[:, head(h)].T for h in range(GROUP)], axis=0)

    def d_score(scores, values):
        weights = jnp.exp2((scores - top) * SCALE)
        d_scores = (weights * (dot(values, d_low_t) - delta)).astype(bf16)
        return weights.astype(bf16), d_scores

    weights, d_scores = d_score(causal_scores(key_ref, query_t_ref[:HD, :]), value_ref[...])
    local_ref[:, :HD] = dot(d_scores, query_s_ref[...]) * FACTOR
    local_ref[:, HD:] = dot(weights, d_low_s)
    total = dot(key_ref[...].T, d_scores)
    for c in range(N_CHUNK):
        rows = slice(c * CHUNK, (c + 1) * CHUNK)
        keys = kv_ref[rows, :HD]
        scores = dot(jnp.concatenate([keys, flag_ref[rows, :]], axis=1), query_t_ref[...])
        _, d_scores = d_score(scores, kv_ref[rows, HD:])
        total = total + dot(keys.T, d_scores)
    part = jnp.zeros((1, ROWS), f32)
    for h in range(GROUP):
        query_grad_ref[:, head(h)] = (total[:, head(h)] * FACTOR).T.astype(bf16)
        grad_t = grad_ref[:, head(h)].astype(f32).T
        part = part + jnp.sum(grad_t * att_t_ref[:, head(h)].astype(f32), axis=0, keepdims=True)
    gate_ref[...] = part
    matrix = owner_matrix(owner_tiles(plan_ref, slot_ref, lax.axis_index("ctx")))
    for c in range(KEYS // HD):
        owner_ref[:, c * HD : (c + 1) * HD] = matrix[c * HD : (c + 1) * HD, :].T


def owner_kernel(owner_ref, returned_ref, local_ref, key_grad_ref, value_grad_ref):
    total = local_ref[...] + dot(owner_ref[...], returned_ref[...])
    key_grad_ref[...] = total[:, :HD].astype(bf16)
    value_grad_ref[...] = total[:, HD:].astype(bf16)


VMEM = pltpu.VMEM
SMEM = pltpu.SMEM
HBM = pltpu.HBM


def call(kernel, ins, outs, scratch, flops, moved, limit=None):
    return pl.pallas_call(
        kernel,
        out_shape=[HBM(shape, kind) if space is HBM else jax.ShapeDtypeStruct(shape, kind) for space, shape, kind in outs],
        in_specs=[pl.BlockSpec(memory_space=space) for space, _ in ins],
        out_specs=[pl.BlockSpec(memory_space=space) for space, _, _ in outs],
        scratch_shapes=scratch,
        compiler_params=pltpu.CompilerParams(vmem_limit_bytes=limit),
        cost_estimate=pl.CostEstimate(flops=flops, bytes_accessed=moved, transcendentals=0),
        interpret=INTERPRET,
        name=kernel.__name__,
    )(*[pltpu.with_memory_space_constraint(array, HBM) if space is HBM else array for space, array in ins])


def exchange(pieces):
    return lax.all_to_all(pieces, "ctx", split_axis=0, concat_axis=0, tiled=True)


def body(queries, key_rows, value_rows, out_grad, gate_logit, tile_plan, mask_kind):
    logit = gate_logit.reshape(1, ROWS)
    plan_row = lax.dynamic_index_in_dim(tile_plan, lax.axis_index("ctx"), 0, keepdims=False)
    (outgoing,) = call(
        send_kernel,
        [(HBM, tile_plan), (HBM, key_rows), (HBM, value_rows)],
        [(HBM, (KEYS, 2 * HD), bf16)],
        [VMEM((PEERS, SECTIONS, PEERS), jnp.int32), VMEM((ROWS, HD), bf16), VMEM((ROWS, HD), bf16),
         VMEM((KEYS, 2 * HD), bf16),
         VMEM((SLOTS, PEERS), f32), pltpu.SemaphoreType.DMA((3 + SEND_PARTS,))],
        2**27, 2**21,
    )
    fetched = exchange(outgoing.reshape(PEERS, SECTIONS, TILE, 2 * HD)).reshape(SLOTS, TILE, 2 * HD)
    query_t, query_s, d_att_t, flags, start, out_t, places, *again = call(
        local_kernel,
        [(SMEM, plan_row), (SMEM, mask_kind[0]), (VMEM, queries), (VMEM, key_rows), (VMEM, value_rows),
         (VMEM, out_grad), (VMEM, logit)],
        [(VMEM, (2 * HD, WIDE), bf16), (VMEM, (WIDE, HD), bf16), (VMEM, (HD, WIDE), bf16), (VMEM, (NEAR, HD), bf16),
         (VMEM, (8, WIDE), f32), (VMEM, (HD, WIDE), f32), (SMEM, (KEPT,), jnp.int32),
         (HBM, (2 * HD, WIDE), bf16), (HBM, (WIDE, HD), bf16), (HBM, (HD, WIDE), bf16), (HBM, (NEAR, HD), bf16)],
        [pltpu.SemaphoreType.DMA((4,))], 2**27, 2**22, limit=VMEM_LIMIT,
    )
    grads, att_t, stat, near = call(
        main_kernel,
        [(VMEM, places), (VMEM, fetched), (VMEM, query_t), (VMEM, flags), (VMEM, start), (VMEM, query_s), (VMEM, d_att_t),
         (VMEM, out_t)],
        [(HBM, (SLOTS, TILE, 2 * HD), bf16), (HBM, (HD, WIDE), bf16), (HBM, (8, WIDE), f32), (HBM, (NEAR, 2 * HD), bf16)],
        [SMEM((KEPT,), jnp.int32), VMEM((SLOTS, TILE, 2 * HD), bf16), VMEM((HD, WIDE), bf16), VMEM((8, WIDE), f32),
         VMEM((NEAR, 2 * HD), bf16),
         VMEM((NEAR, WIDE), f32), VMEM((NEAR, WIDE), bf16), VMEM((NEAR, WIDE), bf16), VMEM((WIDE, HD), bf16),
         pltpu.SemaphoreType.DMA((6,))],
        2**30, 2**22, limit=VMEM_LIMIT,
    )
    returned = exchange(grads.reshape(PEERS, SECTIONS, TILE, 2 * HD)).reshape(KEYS, 2 * HD)
    query_grad, local, gate_part, owner = call(
        query_kernel,
        [(VMEM, tile_plan), (VMEM, near), (VMEM, key_rows), (VMEM, value_rows), (VMEM, out_grad),
         *[(VMEM, array) for array in again], (VMEM, att_t), (VMEM, stat)],
        [(VMEM, (ROWS, WIDE), bf16), (VMEM, (ROWS, 2 * HD), f32), (VMEM, (1, ROWS), f32), (VMEM, (HD, KEYS), bf16)],
        [VMEM((SLOTS, PEERS), f32)],
        2**30, 2**22, limit=VMEM_LIMIT,
    )
    gate = jax.nn.sigmoid(gate_logit)
    gate_sum = lax.all_gather(gate_part[0], "head").sum(0)
    gate_grad = gate * (1.0 - gate) * gate_sum
    key_grad, value_grad = call(
        owner_kernel,
        [(VMEM, owner), (VMEM, returned), (VMEM, local)],
        [(VMEM, (ROWS, HD), bf16), (VMEM, (ROWS, HD), bf16)],
        [], 2**27, 2**21, limit=VMEM_LIMIT,
    )
    return (query_grad, key_grad, value_grad, gate_grad)


def solution(mesh):
    placed = (
        P("ctx", "head"),
        P("ctx", "head"),
        P("ctx", "head"),
        P("ctx", "head"),
        P("ctx"),
        P(),
        P("ctx", None, None),
    )
    return jax.shard_map(
        body,
        mesh=mesh,
        in_specs=placed,
        out_specs=(P("ctx", "head"), P("ctx", "head"), P("ctx", "head"), P("ctx")),
        check_vma=False,
    )
```

```python
import math

import jax
import jax.numpy as jnp
from jax import lax
from jax.experimental import pallas as pl
from jax.experimental.pallas import tpu as pltpu
from jax.sharding import PartitionSpec as P

HD = 128
TILE = 8
SECTIONS = 4
ROWS = 128
PEERS = 64
GROUP = 6
SLOTS = PEERS * SECTIONS
KEYS = SLOTS * TILE
PICKS = 32
KEPT = SECTIONS * PICKS
NEAR = KEPT * TILE
WIDE = GROUP * ROWS
CHUNK = PICKS * TILE
PART = 256
N_CHUNK = NEAR // CHUNK
N_PART = WIDE // PART
SEND_PARTS = 4
FACTOR = 1.0 / math.sqrt(HD)
SCALE = FACTOR * math.log2(math.e)
HIDDEN = -1e30
INTERPRET = False
VMEM_LIMIT = 16 * 2**20

f32 = jnp.float32
bf16 = jnp.bfloat16


def dot(a, b):
    return lax.dot_general(a, b, (((1,), (0,)), ((), ())), preferred_element_type=f32)


def head(h):
    return slice(h * HD, (h + 1) * HD)


def owner_tiles(plan_ref, slot_ref, device):
    for b in range(PEERS):
        slot_ref[b * SECTIONS : (b + 1) * SECTIONS, :] = plan_ref[b].astype(f32)
    pick = (lax.broadcasted_iota(jnp.int32, (PEERS, HD), 0) == device).astype(bf16)
    return dot(slot_ref[...].astype(bf16), pick)


def owner_matrix(tiles):
    column = lax.broadcasted_iota(jnp.int32, (TILE, HD), 1)
    row = lax.broadcasted_iota(jnp.int32, (TILE, HD), 0)
    wanted = jnp.where((column & (TILE - 1)) == row, (column >> 3).astype(f32), -2.0)
    slots = tiles.shape[0]
    wide = jnp.broadcast_to(tiles[:, None, :], (slots, TILE, HD))
    return jnp.where(wide == wanted[None], 1.0, 0.0).reshape(slots * TILE, HD).astype(bf16)


def send_kernel(plan_hbm, key_hbm, value_hbm, out_hbm, plan_ref, key_ref, value_ref, out_ref, slot_ref, sems):
    loads = [
        pltpu.make_async_copy(plan_hbm, plan_ref, sems.at[0]),
        pltpu.make_async_copy(key_hbm, key_ref, sems.at[1]),
        pltpu.make_async_copy(value_hbm, value_ref, sems.at[2]),
    ]
    for load in loads:
        load.start()
    for load in loads:
        load.wait()
    tiles = owner_tiles(plan_ref, slot_ref, lax.axis_index("ctx"))
    both = jnp.concatenate([key_ref[...], value_ref[...]], axis=1)
    stores = []
    for c in range(SEND_PARTS):
        size = KEYS // SEND_PARTS
        matrix = owner_matrix(tiles[c * size // TILE : (c + 1) * size // TILE])
        out_ref[c * size : (c + 1) * size, :] = dot(matrix, both).astype(bf16)
        part = pl.ds(c * size, size)
        stores.append(pltpu.make_async_copy(out_ref.at[part], out_hbm.at[part], sems.at[3 + c]))
        stores[-1].start()
    for store in stores:
        store.wait()


def row_gate(logit_ref):
    return jax.nn.sigmoid(logit_ref[...])


def causal_scores(key_ref, query_t):
    scores = dot(key_ref[...], query_t)
    key_at = lax.broadcasted_iota(jnp.int32, (ROWS, WIDE), 0)
    row_at = lax.broadcasted_iota(jnp.int32, (ROWS, WIDE), 1) & (ROWS - 1)
    return jnp.where(row_at >= key_at, scores, HIDDEN)


def local_kernel(
    plan_ref, kind_ref, query_ref, key_ref, value_ref, grad_ref, logit_ref,
    query_t_ref, query_s_ref, d_att_t_ref, flag_ref, start_ref, out_t_ref, list_ref,
    query_t_hbm, query_s_hbm, d_att_t_hbm, flag_hbm, sems,
):
    gate = row_gate(logit_ref)
    for h in range(GROUP):
        block = query_ref[:, head(h)]
        query_s_ref[head(h), :] = block
        query_t_ref[:HD, head(h)] = block.astype(f32).T.astype(bf16)
        grad_t = grad_ref[:, head(h)].astype(f32).T
        d_att_t_ref[:, head(h)] = (gate * grad_t).astype(bf16)
    scores = causal_scores(key_ref, query_t_ref[:HD, :])
    top = jnp.max(scores, axis=0, keepdims=True)
    weights = jnp.exp2((scores - top) * SCALE)
    start_ref[0:1, :] = top
    start_ref[1:2, :] = jnp.sum(weights, axis=0, keepdims=True)
    value_t = value_ref[...].astype(f32).T.astype(bf16)
    out_t_ref[...] = dot(value_t, weights.astype(bf16))
    device = lax.axis_index("ctx")
    flag = lax.broadcasted_iota(jnp.int32, (HD, WIDE), 0)
    early = (lax.broadcasted_iota(jnp.int32, (HD, WIDE), 1) & (ROWS - 1)) < ROWS // 2
    query_t_ref[HD:, :] = jnp.where((flag == 0) | ((flag == 1) & early), HIDDEN, 0.0).astype(bf16)
    lane = lax.broadcasted_iota(jnp.int32, (TILE, HD), 1)
    flag_ref[...] = (lax.broadcasted_iota(jnp.int32, (NEAR, HD), 1) == 0).astype(bf16)
    for s in range(SECTIONS):

        @pl.loop(0, PICKS)
        def _(k):
            list_ref[s * PICKS + k] = device

        def place(p, count):
            given = plan_ref[s, p] >= 0

            @pl.when(given)
            def _():
                list_ref[s * PICKS + count] = p
                at = pl.multiple_of((s * PICKS + count) * TILE, TILE)
                chosen = jnp.where(kind_ref[s, p] == 0, -1, 1)
                flag_ref[pl.ds(at, TILE), :] = (lane == chosen).astype(bf16)

            return count + given.astype(jnp.int32)

        lax.fori_loop(0, PEERS, place, jnp.int32(0))
    sources = (query_t_ref, query_s_ref, d_att_t_ref, flag_ref)
    copies = (query_t_hbm, query_s_hbm, d_att_t_hbm, flag_hbm)
    stores = [
        pltpu.make_async_copy(source, copy, sems.at[n])
        for n, (source, copy) in enumerate(zip(sources, copies, strict=True))
    ]
    for store in stores:
        store.start()
    for store in stores:
        store.wait()


def main_kernel(
    list_in_ref, slots_ref, query_t_ref, flag_ref, start_ref, query_s_ref, d_att_t_ref, out_t_ref,
    grad_hbm, att_t_hbm, stat_hbm, kv_hbm,
    list_ref, grad_ref, att_t_ref, stat_ref, kv_ref, score_ref, weight_ref, d_score_ref, d_low_ref, sems,
):
    load = pltpu.make_async_copy(list_in_ref, list_ref, sems.at[3])
    load.start()
    grad_ref[...] = jnp.zeros_like(grad_ref)
    load.wait()
    for k in range(KEPT):
        kv_ref[k * TILE : (k + 1) * TILE, :] = slots_ref[list_ref[k], k // PICKS]
    value_t = kv_ref[:, HD:].T
    chunks = [slice(c * CHUNK, (c + 1) * CHUNK) for c in range(N_CHUNK)]
    parts = [slice(n * PART, (n + 1) * PART) for n in range(N_PART)]
    tops, totals, outs, deltas, lows = [], [], [], [], []

    def score(n):
        top = jnp.broadcast_to(start_ref[0:1, parts[n]], (TILE, PART))
        for rows in chunks:
            keys = jnp.concatenate([kv_ref[rows, :HD], flag_ref[rows, :]], axis=1)
            scores = dot(keys, query_t_ref[:, parts[n]])
            score_ref[rows, parts[n]] = scores
            top = jnp.maximum(top, jnp.max(scores.reshape(CHUNK // TILE, TILE, PART), axis=0))
        tops.append(jnp.max(top, axis=0, keepdims=True))

    def weigh(n):
        total = jnp.zeros((TILE, PART), f32)
        for c in range(NEAR // 32):
            rows = slice(c * 32, (c + 1) * 32)
            weights = jnp.exp2((score_ref[rows, parts[n]] - tops[n]) * SCALE)
            total = total + jnp.sum(weights.reshape(32 // TILE, TILE, PART), axis=0)
            weight_ref[rows, parts[n]] = weights.astype(bf16)
        totals.append(jnp.sum(total, axis=0, keepdims=True))
        outs.append(dot(value_t, weight_ref[:, parts[n]]))

    def finish(n):
        share = jnp.exp2((start_ref[0:1, parts[n]] - tops[n]) * SCALE)
        inverse = 1.0 / (totals[n] + share * start_ref[1:2, parts[n]])
        att_t = ((outs[n] + share * out_t_ref[:, parts[n]]) * inverse).astype(bf16)
        att_t_ref[:, parts[n]] = att_t
        d_att_t = d_att_t_ref[:, parts[n]].astype(f32)
        deltas.append(jnp.sum(d_att_t * att_t.astype(f32), axis=0, keepdims=True) * inverse)
        lows.append((d_att_t * inverse).astype(bf16))
        for h in range(PART // HD):
            at = n * PART + h * HD
            d_low_ref[at : at + HD, :] = lows[n][:, head(h)].T
        stat_ref[0:1, parts[n]] = tops[n]
        stat_ref[1:2, parts[n]] = inverse
        stat_ref[2:3, parts[n]] = deltas[n]

    def back(n):
        for rows in chunks:
            d_probs = dot(kv_ref[rows, HD:], lows[n])
            weights = weight_ref[rows, parts[n]].astype(f32)
            d_score_ref[rows, parts[n]] = (weights * (d_probs - deltas[n])).astype(bf16)

    score(0)
    for n in range(N_PART):
        if n + 1 < N_PART:
            score(n + 1)
        weigh(n)
        if n > 0:
            back(n - 1)
        finish(n)
    stores = [
        pltpu.make_async_copy(kv_ref, kv_hbm, sems.at[0]),
        pltpu.make_async_copy(att_t_ref, att_t_hbm, sems.at[1]),
        pltpu.make_async_copy(stat_ref, stat_hbm, sems.at[2]),
    ]
    for store in stores:
        store.start()

    def scatter(values, s, side):
        for k in range(PICKS):
            block = list_ref[s * PICKS + k]
            grad_ref[block, s, :, side * HD : (side + 1) * HD] = values[k * TILE : (k + 1) * TILE, :]

    for s in range(SECTIONS):
        scatter(dot(weight_ref[chunks[s], :], d_low_ref[...]).astype(bf16), s, 1)
    back(N_PART - 1)
    for s in range(SECTIONS):
        scatter((dot(d_score_ref[chunks[s], :], query_s_ref[...]) * FACTOR).astype(bf16), s, 0)
        stores.append(pltpu.make_async_copy(grad_ref.at[:, s], grad_hbm.at[:, s], sems.at[4 + s]))
        stores[-1].start()
    for store in stores:
        store.wait()


def query_kernel(
    plan_ref, kv_ref, key_ref, value_ref, grad_ref, query_t_ref, query_s_ref, d_att_t_ref, flag_ref,
    att_t_ref, stat_ref, query_grad_ref, local_ref, gate_ref, owner_ref, slot_ref,
):
    top, inverse, delta = stat_ref[0:1, :], stat_ref[1:2, :], stat_ref[2:3, :]
    d_low_t = (d_att_t_ref[...].astype(f32) * inverse).astype(bf16)
    d_low_s = jnp.concatenate([d_low_t[:, head(h)].T for h in range(GROUP)], axis=0)

    def d_score(scores, values):
        weights = jnp.exp2((scores - top) * SCALE)
        d_scores = (weights * (dot(values, d_low_t) - delta)).astype(bf16)
        return weights.astype(bf16), d_scores

    weights, d_scores = d_score(causal_scores(key_ref, query_t_ref[:HD, :]), value_ref[...])
    local_ref[:, :HD] = dot(d_scores, query_s_ref[...]) * FACTOR
    local_ref[:, HD:] = dot(weights, d_low_s)
    total = dot(key_ref[...].T, d_scores)
    for c in range(N_CHUNK):
        rows = slice(c * CHUNK, (c + 1) * CHUNK)
        keys = kv_ref[rows, :HD]
        scores = dot(jnp.concatenate([keys, flag_ref[rows, :]], axis=1), query_t_ref[...])
        _, d_scores = d_score(scores, kv_ref[rows, HD:])
        total = total + dot(keys.T, d_scores)
    part = jnp.zeros((1, ROWS), f32)
    for h in range(GROUP):
        query_grad_ref[:, head(h)] = (total[:, head(h)] * FACTOR).T.astype(bf16)
        grad_t = grad_ref[:, head(h)].astype(f32).T
        part = part + jnp.sum(grad_t * att_t_ref[:, head(h)].astype(f32), axis=0, keepdims=True)
    gate_ref[...] = part
    matrix = owner_matrix(owner_tiles(plan_ref, slot_ref, lax.axis_index("ctx")))
    for c in range(KEYS // HD):
        owner_ref[:, c * HD : (c + 1) * HD] = matrix[c * HD : (c + 1) * HD, :].T


def owner_kernel(owner_ref, returned_ref, local_ref, key_grad_ref, value_grad_ref):
    total = local_ref[...] + dot(owner_ref[...], returned_ref[...])
    key_grad_ref[...] = total[:, :HD].astype(bf16)
    value_grad_ref[...] = total[:, HD:].astype(bf16)


VMEM = pltpu.VMEM
SMEM = pltpu.SMEM
HBM = pltpu.HBM


def call(kernel, ins, outs, scratch, flops, moved, limit=None):
    return pl.pallas_call(
        kernel,
        out_shape=[HBM(shape, kind) if space is HBM else jax.ShapeDtypeStruct(shape, kind) for space, shape, kind in outs],
        in_specs=[pl.BlockSpec(memory_space=space) for space, _ in ins],
        out_specs=[pl.BlockSpec(memory_space=space) for space, _, _ in outs],
        scratch_shapes=scratch,
        compiler_params=pltpu.CompilerParams(vmem_limit_bytes=limit),
        cost_estimate=pl.CostEstimate(flops=flops, bytes_accessed=moved, transcendentals=0),
        interpret=INTERPRET,
        name=kernel.__name__,
    )(*[pltpu.with_memory_space_constraint(array, HBM) if space is HBM else array for space, array in ins])


def exchange(pieces):
    return lax.all_to_all(pieces, "ctx", split_axis=0, concat_axis=0, tiled=True)


def body(queries, key_rows, value_rows, out_grad, gate_logit, tile_plan, mask_kind):
    logit = gate_logit.reshape(1, ROWS)
    plan_row = lax.dynamic_index_in_dim(tile_plan, lax.axis_index("ctx"), 0, keepdims=False)
    (outgoing,) = call(
        send_kernel,
        [(HBM, tile_plan), (HBM, key_rows), (HBM, value_rows)],
        [(HBM, (KEYS, 2 * HD), bf16)],
        [VMEM((PEERS, SECTIONS, PEERS), jnp.int32), VMEM((ROWS, HD), bf16), VMEM((ROWS, HD), bf16),
         VMEM((KEYS, 2 * HD), bf16),
         VMEM((SLOTS, PEERS), f32), pltpu.SemaphoreType.DMA((3 + SEND_PARTS,))],
        2**27, 2**21,
    )
    fetched = exchange(outgoing.reshape(PEERS, SECTIONS, TILE, 2 * HD))
    query_t, query_s, d_att_t, flags, start, out_t, places, *again = call(
        local_kernel,
        [(SMEM, plan_row), (SMEM, mask_kind[0]), (VMEM, queries), (VMEM, key_rows), (VMEM, value_rows),
         (VMEM, out_grad), (VMEM, logit)],
        [(VMEM, (2 * HD, WIDE), bf16), (VMEM, (WIDE, HD), bf16), (VMEM, (HD, WIDE), bf16), (VMEM, (NEAR, HD), bf16),
         (VMEM, (8, WIDE), f32), (VMEM, (HD, WIDE), f32), (SMEM, (KEPT,), jnp.int32),
         (HBM, (2 * HD, WIDE), bf16), (HBM, (WIDE, HD), bf16), (HBM, (HD, WIDE), bf16), (HBM, (NEAR, HD), bf16)],
        [pltpu.SemaphoreType.DMA((4,))], 2**27, 2**22, limit=VMEM_LIMIT,
    )
    grads, att_t, stat, near = call(
        main_kernel,
        [(VMEM, places), (VMEM, fetched), (VMEM, query_t), (VMEM, flags), (VMEM, start), (VMEM, query_s), (VMEM, d_att_t),
         (VMEM, out_t)],
        [(HBM, (PEERS, SECTIONS, TILE, 2 * HD), bf16), (HBM, (HD, WIDE), bf16), (HBM, (8, WIDE), f32),
         (HBM, (NEAR, 2 * HD), bf16)],
        [SMEM((KEPT,), jnp.int32), VMEM((PEERS, SECTIONS, TILE, 2 * HD), bf16), VMEM((HD, WIDE), bf16), VMEM((8, WIDE), f32),
         VMEM((NEAR, 2 * HD), bf16),
         VMEM((NEAR, WIDE), f32), VMEM((NEAR, WIDE), bf16), VMEM((NEAR, WIDE), bf16), VMEM((WIDE, HD), bf16),
         pltpu.SemaphoreType.DMA((8,))],
        2**30, 2**22, limit=VMEM_LIMIT,
    )
    returned = exchange(grads).reshape(KEYS, 2 * HD)
    query_grad, local, gate_part, owner = call(
        query_kernel,
        [(VMEM, tile_plan), (VMEM, near), (VMEM, key_rows), (VMEM, value_rows), (VMEM, out_grad),
         *[(VMEM, array) for array in again], (VMEM, att_t), (VMEM, stat)],
        [(VMEM, (ROWS, WIDE), bf16), (VMEM, (ROWS, 2 * HD), f32), (VMEM, (1, ROWS), f32), (VMEM, (HD, KEYS), bf16)],
        [VMEM((SLOTS, PEERS), f32)],
        2**30, 2**22, limit=VMEM_LIMIT,
    )
    gate = jax.nn.sigmoid(gate_logit)
    gate_sum = lax.all_gather(gate_part[0], "head").sum(0)
    gate_grad = gate * (1.0 - gate) * gate_sum
    key_grad, value_grad = call(
        owner_kernel,
        [(VMEM, owner), (VMEM, returned), (VMEM, local)],
        [(VMEM, (ROWS, HD), bf16), (VMEM, (ROWS, HD), bf16)],
        [], 2**27, 2**21, limit=VMEM_LIMIT,
    )
    return (query_grad, key_grad, value_grad, gate_grad)


def solution(mesh):
    placed = (
        P("ctx", "head"),
        P("ctx", "head"),
        P("ctx", "head"),
        P("ctx", "head"),
        P("ctx"),
        P(),
        P("ctx", None, None),
    )
    return jax.shard_map(
        body,
        mesh=mesh,
        in_specs=placed,
        out_specs=(P("ctx", "head"), P("ctx", "head"), P("ctx", "head"), P("ctx")),
        check_vma=False,
    )
```

```python
import math

import jax
import jax.numpy as jnp
from jax import lax
from jax.experimental import pallas as pl
from jax.experimental.pallas import tpu as pltpu
from jax.sharding import PartitionSpec as P

HD = 128
TILE = 8
SECTIONS = 4
ROWS = 128
PEERS = 64
GROUP = 6
SLOTS = PEERS * SECTIONS
KEYS = SLOTS * TILE
PICKS = 32
KEPT = SECTIONS * PICKS
NEAR = KEPT * TILE
WIDE = GROUP * ROWS
CHUNK = PICKS * TILE
PART = 256
N_CHUNK = NEAR // CHUNK
N_PART = WIDE // PART
SEND_PARTS = 4
FACTOR = 1.0 / math.sqrt(HD)
SCALE = FACTOR * math.log2(math.e)
HIDDEN = -1e30
INTERPRET = False
VMEM_LIMIT = 16 * 2**20

f32 = jnp.float32
bf16 = jnp.bfloat16


def dot(a, b):
    return lax.dot_general(a, b, (((1,), (0,)), ((), ())), preferred_element_type=f32)


def head(h):
    return slice(h * HD, (h + 1) * HD)


def owner_tiles(plan_ref, slot_ref, device):
    for b in range(PEERS):
        slot_ref[b * SECTIONS : (b + 1) * SECTIONS, :] = plan_ref[b].astype(f32)
    pick = (lax.broadcasted_iota(jnp.int32, (PEERS, HD), 0) == device).astype(bf16)
    return dot(slot_ref[...].astype(bf16), pick)


def owner_matrix(tiles):
    column = lax.broadcasted_iota(jnp.int32, (TILE, HD), 1)
    row = lax.broadcasted_iota(jnp.int32, (TILE, HD), 0)
    wanted = jnp.where((column & (TILE - 1)) == row, (column >> 3).astype(f32), -2.0)
    slots = tiles.shape[0]
    wide = jnp.broadcast_to(tiles[:, None, :], (slots, TILE, HD))
    return jnp.where(wide == wanted[None], 1.0, 0.0).reshape(slots * TILE, HD).astype(bf16)


def send_kernel(plan_hbm, key_hbm, value_hbm, out_hbm, plan_ref, key_ref, value_ref, out_ref, slot_ref, sems):
    loads = [
        pltpu.make_async_copy(plan_hbm, plan_ref, sems.at[0]),
        pltpu.make_async_copy(key_hbm, key_ref, sems.at[1]),
        pltpu.make_async_copy(value_hbm, value_ref, sems.at[2]),
    ]
    for load in loads:
        load.start()
    for load in loads:
        load.wait()
    tiles = owner_tiles(plan_ref, slot_ref, lax.axis_index("ctx"))
    both = jnp.concatenate([key_ref[...], value_ref[...]], axis=1)
    stores = []
    for c in range(SEND_PARTS):
        size = KEYS // SEND_PARTS
        matrix = owner_matrix(tiles[c * size // TILE : (c + 1) * size // TILE])
        out_ref[c * size : (c + 1) * size, :] = dot(matrix, both).astype(bf16)
        part = pl.ds(c * size, size)
        stores.append(pltpu.make_async_copy(out_ref.at[part], out_hbm.at[part], sems.at[3 + c]))
        stores[-1].start()
    for store in stores:
        store.wait()


def row_gate(logit_ref):
    return jax.nn.sigmoid(logit_ref[...])


def causal_scores(key_ref, query_t):
    scores = dot(key_ref[...], query_t)
    key_at = lax.broadcasted_iota(jnp.int32, (ROWS, WIDE), 0)
    row_at = lax.broadcasted_iota(jnp.int32, (ROWS, WIDE), 1) & (ROWS - 1)
    return jnp.where(row_at >= key_at, scores, HIDDEN)


def local_kernel(
    plan_ref, kind_ref, query_ref, key_ref, value_ref, grad_ref, logit_ref,
    query_t_ref, query_s_ref, d_att_t_ref, flag_ref, start_ref, out_t_ref, list_ref,
    query_t_hbm, query_s_hbm, d_att_t_hbm, flag_hbm, sems,
):
    gate = row_gate(logit_ref)
    for h in range(GROUP):
        block = query_ref[:, head(h)]
        query_s_ref[head(h), :] = block
        query_t_ref[:HD, head(h)] = block.astype(f32).T.astype(bf16)
        grad_t = grad_ref[:, head(h)].astype(f32).T
        d_att_t_ref[:, head(h)] = (gate * grad_t).astype(bf16)
    scores = causal_scores(key_ref, query_t_ref[:HD, :])
    top = jnp.max(scores, axis=0, keepdims=True)
    weights = jnp.exp2((scores - top) * SCALE)
    start_ref[0:1, :] = top
    start_ref[1:2, :] = jnp.sum(weights, axis=0, keepdims=True)
    value_t = value_ref[...].astype(f32).T.astype(bf16)
    out_t_ref[...] = dot(value_t, weights.astype(bf16))
    device = lax.axis_index("ctx")
    flag = lax.broadcasted_iota(jnp.int32, (HD, WIDE), 0)
    early = (lax.broadcasted_iota(jnp.int32, (HD, WIDE), 1) & (ROWS - 1)) < ROWS // 2
    query_t_ref[HD:, :] = jnp.where((flag == 0) | ((flag == 1) & early), HIDDEN, 0.0).astype(bf16)
    lane = lax.broadcasted_iota(jnp.int32, (TILE, HD), 1)
    flag_ref[...] = (lax.broadcasted_iota(jnp.int32, (NEAR, HD), 1) == 0).astype(bf16)
    for s in range(SECTIONS):

        @pl.loop(0, PICKS)
        def _(k):
            list_ref[s * PICKS + k] = device

        def place(p, count):
            given = plan_ref[s, p] >= 0

            @pl.when(given)
            def _():
                list_ref[s * PICKS + count] = p
                at = pl.multiple_of((s * PICKS + count) * TILE, TILE)
                chosen = jnp.where(kind_ref[s, p] == 0, -1, 1)
                flag_ref[pl.ds(at, TILE), :] = (lane == chosen).astype(bf16)

            return count + given.astype(jnp.int32)

        lax.fori_loop(0, PEERS, place, jnp.int32(0))
    sources = (query_t_ref, query_s_ref, d_att_t_ref, flag_ref)
    copies = (query_t_hbm, query_s_hbm, d_att_t_hbm, flag_hbm)
    stores = [
        pltpu.make_async_copy(source, copy, sems.at[n])
        for n, (source, copy) in enumerate(zip(sources, copies, strict=True))
    ]
    for store in stores:
        store.start()
    for store in stores:
        store.wait()


def main_kernel(
    list_in_ref, slots_ref, query_t_ref, flag_ref, start_ref, query_s_ref, d_att_t_ref, out_t_ref,
    grad_hbm, att_t_hbm, stat_hbm, kv_hbm,
    list_ref, grad_ref, att_t_ref, stat_ref, kv_ref, score_ref, weight_ref, d_score_ref, d_low_ref, sems,
):
    load = pltpu.make_async_copy(list_in_ref, list_ref, sems.at[3])
    load.start()
    grad_ref[...] = jnp.zeros_like(grad_ref)
    load.wait()
    for k in range(KEPT):
        kv_ref[k * TILE : (k + 1) * TILE, :] = slots_ref[list_ref[k], k // PICKS]
    value_t = kv_ref[:, HD:].T
    chunks = [slice(c * CHUNK, (c + 1) * CHUNK) for c in range(N_CHUNK)]
    parts = [slice(n * PART, (n + 1) * PART) for n in range(N_PART)]
    tops, totals, outs, deltas, lows = [], [], [], [], []

    def score(n):
        top = jnp.broadcast_to(start_ref[0:1, parts[n]], (TILE, PART))
        for rows in chunks:
            keys = jnp.concatenate([kv_ref[rows, :HD], flag_ref[rows, :]], axis=1)
            scores = dot(keys, query_t_ref[:, parts[n]])
            score_ref[rows, parts[n]] = scores
            top = jnp.maximum(top, jnp.max(scores.reshape(CHUNK // TILE, TILE, PART), axis=0))
        tops.append(jnp.max(top, axis=0, keepdims=True))

    def weigh(n):
        total = jnp.zeros((TILE, PART), f32)
        for c in range(NEAR // 32):
            rows = slice(c * 32, (c + 1) * 32)
            weights = jnp.exp2((score_ref[rows, parts[n]] - tops[n]) * SCALE)
            total = total + jnp.sum(weights.reshape(32 // TILE, TILE, PART), axis=0)
            weight_ref[rows, parts[n]] = weights.astype(bf16)
        totals.append(jnp.sum(total, axis=0, keepdims=True))
        outs.append(dot(value_t, weight_ref[:, parts[n]]))

    def finish(n):
        share = jnp.exp2((start_ref[0:1, parts[n]] - tops[n]) * SCALE)
        inverse = 1.0 / (totals[n] + share * start_ref[1:2, parts[n]])
        att_t = ((outs[n] + share * out_t_ref[:, parts[n]]) * inverse).astype(bf16)
        att_t_ref[:, parts[n]] = att_t
        d_att_t = d_att_t_ref[:, parts[n]].astype(f32)
        deltas.append(jnp.sum(d_att_t * att_t.astype(f32), axis=0, keepdims=True) * inverse)
        lows.append((d_att_t * inverse).astype(bf16))
        for h in range(PART // HD):
            at = n * PART + h * HD
            d_low_ref[at : at + HD, :] = lows[n][:, head(h)].T
        stat_ref[0:1, parts[n]] = tops[n]
        stat_ref[1:2, parts[n]] = inverse
        stat_ref[2:3, parts[n]] = deltas[n]

    def back(n):
        for rows in chunks:
            d_probs = dot(kv_ref[rows, HD:], lows[n])
            weights = weight_ref[rows, parts[n]].astype(f32)
            d_score_ref[rows, parts[n]] = (weights * (d_probs - deltas[n])).astype(bf16)

    score(0)
    for n in range(N_PART):
        if n + 1 < N_PART:
            score(n + 1)
        weigh(n)
        finish(n)
        if n > 0:
            back(n - 1)
    stores = [
        pltpu.make_async_copy(kv_ref, kv_hbm, sems.at[0]),
        pltpu.make_async_copy(att_t_ref, att_t_hbm, sems.at[1]),
        pltpu.make_async_copy(stat_ref, stat_hbm, sems.at[2]),
    ]
    for store in stores:
        store.start()

    def scatter(values, s, side):
        for k in range(PICKS):
            block = list_ref[s * PICKS + k]
            grad_ref[block, s, :, side * HD : (side + 1) * HD] = values[k * TILE : (k + 1) * TILE, :]

    back(N_PART - 1)
    for s in range(SECTIONS):
        scatter(dot(weight_ref[chunks[s], :], d_low_ref[...]).astype(bf16), s, 1)
    for s in range(SECTIONS):
        scatter((dot(d_score_ref[chunks[s], :], query_s_ref[...]) * FACTOR).astype(bf16), s, 0)
        stores.append(pltpu.make_async_copy(grad_ref.at[:, s], grad_hbm.at[:, s], sems.at[4 + s]))
        stores[-1].start()
    for store in stores:
        store.wait()


def query_kernel(
    plan_ref, kv_ref, key_ref, value_ref, grad_ref, query_t_ref, query_s_ref, d_att_t_ref, flag_ref,
    att_t_ref, stat_ref, query_grad_ref, local_ref, gate_ref, owner_ref, slot_ref,
):
    top, inverse, delta = stat_ref[0:1, :], stat_ref[1:2, :], stat_ref[2:3, :]
    d_low_t = (d_att_t_ref[...].astype(f32) * inverse).astype(bf16)
    d_low_s = jnp.concatenate([d_low_t[:, head(h)].T for h in range(GROUP)], axis=0)

    def d_score(scores, values):
        weights = jnp.exp2((scores - top) * SCALE)
        d_scores = (weights * (dot(values, d_low_t) - delta)).astype(bf16)
        return weights.astype(bf16), d_scores

    weights, d_scores = d_score(causal_scores(key_ref, query_t_ref[:HD, :]), value_ref[...])
    local_ref[:, :HD] = dot(d_scores, query_s_ref[...]) * FACTOR
    local_ref[:, HD:] = dot(weights, d_low_s)
    total = dot(key_ref[...].T, d_scores)
    for c in range(N_CHUNK):
        rows = slice(c * CHUNK, (c + 1) * CHUNK)
        keys = kv_ref[rows, :HD]
        scores = dot(jnp.concatenate([keys, flag_ref[rows, :]], axis=1), query_t_ref[...])
        _, d_scores = d_score(scores, kv_ref[rows, HD:])
        total = total + dot(keys.T, d_scores)
    part = jnp.zeros((1, ROWS), f32)
    for h in range(GROUP):
        query_grad_ref[:, head(h)] = (total[:, head(h)] * FACTOR).T.astype(bf16)
        grad_t = grad_ref[:, head(h)].astype(f32).T
        part = part + jnp.sum(grad_t * att_t_ref[:, head(h)].astype(f32), axis=0, keepdims=True)
    gate_ref[...] = part
    matrix = owner_matrix(owner_tiles(plan_ref, slot_ref, lax.axis_index("ctx")))
    for c in range(KEYS // HD):
        owner_ref[:, c * HD : (c + 1) * HD] = matrix[c * HD : (c + 1) * HD, :].T


def owner_kernel(owner_ref, returned_ref, local_ref, key_grad_ref, value_grad_ref):
    total = local_ref[...] + dot(owner_ref[...], returned_ref[...])
    key_grad_ref[...] = total[:, :HD].astype(bf16)
    value_grad_ref[...] = total[:, HD:].astype(bf16)


VMEM = pltpu.VMEM
SMEM = pltpu.SMEM
HBM = pltpu.HBM


def call(kernel, ins, outs, scratch, flops, moved, limit=None):
    return pl.pallas_call(
        kernel,
        out_shape=[HBM(shape, kind) if space is HBM else jax.ShapeDtypeStruct(shape, kind) for space, shape, kind in outs],
        in_specs=[pl.BlockSpec(memory_space=space) for space, _ in ins],
        out_specs=[pl.BlockSpec(memory_space=space) for space, _, _ in outs],
        scratch_shapes=scratch,
        compiler_params=pltpu.CompilerParams(vmem_limit_bytes=limit),
        cost_estimate=pl.CostEstimate(flops=flops, bytes_accessed=moved, transcendentals=0),
        interpret=INTERPRET,
        name=kernel.__name__,
    )(*[pltpu.with_memory_space_constraint(array, HBM) if space is HBM else array for space, array in ins])


def exchange(pieces):
    return lax.all_to_all(pieces, "ctx", split_axis=0, concat_axis=0, tiled=True)


def body(queries, key_rows, value_rows, out_grad, gate_logit, tile_plan, mask_kind):
    logit = gate_logit.reshape(1, ROWS)
    plan_row = lax.dynamic_index_in_dim(tile_plan, lax.axis_index("ctx"), 0, keepdims=False)
    (outgoing,) = call(
        send_kernel,
        [(HBM, tile_plan), (HBM, key_rows), (HBM, value_rows)],
        [(HBM, (KEYS, 2 * HD), bf16)],
        [VMEM((PEERS, SECTIONS, PEERS), jnp.int32), VMEM((ROWS, HD), bf16), VMEM((ROWS, HD), bf16),
         VMEM((KEYS, 2 * HD), bf16),
         VMEM((SLOTS, PEERS), f32), pltpu.SemaphoreType.DMA((3 + SEND_PARTS,))],
        2**27, 2**21,
    )
    fetched = exchange(outgoing.reshape(PEERS, SECTIONS, TILE, 2 * HD))
    query_t, query_s, d_att_t, flags, start, out_t, places, *again = call(
        local_kernel,
        [(SMEM, plan_row), (SMEM, mask_kind[0]), (VMEM, queries), (VMEM, key_rows), (VMEM, value_rows),
         (VMEM, out_grad), (VMEM, logit)],
        [(VMEM, (2 * HD, WIDE), bf16), (VMEM, (WIDE, HD), bf16), (VMEM, (HD, WIDE), bf16), (VMEM, (NEAR, HD), bf16),
         (VMEM, (8, WIDE), f32), (VMEM, (HD, WIDE), f32), (SMEM, (KEPT,), jnp.int32),
         (HBM, (2 * HD, WIDE), bf16), (HBM, (WIDE, HD), bf16), (HBM, (HD, WIDE), bf16), (HBM, (NEAR, HD), bf16)],
        [pltpu.SemaphoreType.DMA((4,))], 2**27, 2**22, limit=VMEM_LIMIT,
    )
    grads, att_t, stat, near = call(
        main_kernel,
        [(VMEM, places), (VMEM, fetched), (VMEM, query_t), (VMEM, flags), (VMEM, start), (VMEM, query_s), (VMEM, d_att_t),
         (VMEM, out_t)],
        [(HBM, (PEERS, SECTIONS, TILE, 2 * HD), bf16), (HBM, (HD, WIDE), bf16), (HBM, (8, WIDE), f32),
         (HBM, (NEAR, 2 * HD), bf16)],
        [SMEM((KEPT,), jnp.int32), VMEM((PEERS, SECTIONS, TILE, 2 * HD), bf16), VMEM((HD, WIDE), bf16), VMEM((8, WIDE), f32),
         VMEM((NEAR, 2 * HD), bf16),
         VMEM((NEAR, WIDE), f32), VMEM((NEAR, WIDE), bf16), VMEM((NEAR, WIDE), bf16), VMEM((WIDE, HD), bf16),
         pltpu.SemaphoreType.DMA((8,))],
        2**30, 2**22, limit=VMEM_LIMIT,
    )
    returned = exchange(grads).reshape(KEYS, 2 * HD)
    query_grad, local, gate_part, owner = call(
        query_kernel,
        [(VMEM, tile_plan), (VMEM, near), (VMEM, key_rows), (VMEM, value_rows), (VMEM, out_grad),
         *[(VMEM, array) for array in again], (VMEM, att_t), (VMEM, stat)],
        [(VMEM, (ROWS, WIDE), bf16), (VMEM, (ROWS, 2 * HD), f32), (VMEM, (1, ROWS), f32), (VMEM, (HD, KEYS), bf16)],
        [VMEM((SLOTS, PEERS), f32)],
        2**30, 2**22, limit=VMEM_LIMIT,
    )
    gate = jax.nn.sigmoid(gate_logit)
    gate_sum = lax.all_gather(gate_part[0], "head").sum(0)
    gate_grad = gate * (1.0 - gate) * gate_sum
    key_grad, value_grad = call(
        owner_kernel,
        [(VMEM, owner), (VMEM, returned), (VMEM, local)],
        [(VMEM, (ROWS, HD), bf16), (VMEM, (ROWS, HD), bf16)],
        [], 2**27, 2**21, limit=VMEM_LIMIT,
    )
    return (query_grad, key_grad, value_grad, gate_grad)


def solution(mesh):
    placed = (
        P("ctx", "head"),
        P("ctx", "head"),
        P("ctx", "head"),
        P("ctx", "head"),
        P("ctx"),
        P(),
        P("ctx", None, None),
    )
    return jax.shard_map(
        body,
        mesh=mesh,
        in_specs=placed,
        out_specs=(P("ctx", "head"), P("ctx", "head"), P("ctx", "head"), P("ctx")),
        check_vma=False,
    )
```
